512 devices in a mesh: sub: 64 (over y, z), crow: 4 (over x_lo, core), ccol: 2 (over x_hi).
Axes of the slice: x: 4 (x_hi: 2, x_lo: 2; x = x_hi * 2 + x_lo), y: 8, z: 8, core: 2. Of those that a mesh axis runs over, the one named last changes fastest.
Arguments:
- loads: bfloat16 [128, 1024, 128], P('sub'), may hold values from -6 to 6
- stiffness: bfloat16 [128, 1024, 1024], P('sub', ('crow', 'ccol'))
- local_inverse: bfloat16 [128, 1024, 1024], P('sub', ('crow', 'ccol'))
- coarse_basis: bfloat16 [128, 1024, 48], P('sub', ('crow', 'ccol')), may hold values from -0.1875 to 0.1875
- coarse_inverse: bfloat16 [6144, 6144], P('sub', ('crow', 'ccol'))
- coarse_index: int32 [128, 48], P('sub'), may hold values from 0 to 6143, as said below
- left_rows: int32 [128, 128], P('sub'), may hold values from 0 to 1023, as said below
- right_rows: int32 [128, 128], P('sub'), may hold values from 0 to 1023, as said below
Outputs:
- second_pass: float32 [128, 1024, 128], P('sub', ('crow', 'ccol'))
- final_residual: float32 [128, 1024, 128], P('sub', ('crow', 'ccol'))
The draws below stay inside these ranges and needn't reach their ends.
Inputs may be any that keep to these rules, and one draw needn't show every extreme that they name: `coarse_index`: every value 0 to 6143 appears exactly once in the whole array. Of the 96 values in the rows of one index of sub, at most 24 lie in one block of 768 consecutive coarse rows starting at a multiple of 768, and that most is reached. In each subdomain the 128 entries of left_rows and the 128 entries of right_rows are 256 distinct rows. `right_rows`: see left_rows.
All inputs are finite; a program needn't handle non-finite values.
Results may differ from the reference program's by a relative error of at most 0.0067.
Values may be sent and summed in bfloat16 or wider, within the bound.
A program may use at most 64 MiB of HBM per device.

```python
import math
import jax
import jax.numpy as jnp
from jax import lax

IFACE = 1024
FACE = 128
MODES = 48
SUB_DEV = 2
CASES = 128
NSUB = 128
NC = 6144
N_SUB = 64
N_CROW = 4
N_CCOL = 2


def dominant_matrices(key, count, order, low, high, spread):
    key_off, key_diag = jax.random.split(jax.random.fold_in(key, 11))
    off_diag = jax.random.normal(key_off, (count, order, order), jnp.float32) * (spread / math.sqrt(order))
    diagonal = jax.random.uniform(key_diag, (count, order), jnp.float32, low, high)
    return off_diag + diagonal[:, :, None] * jnp.eye(order, dtype=jnp.float32)[None, :, :]


def draw_stiffness(key, part):
    return dominant_matrices(jax.random.fold_in(key, 1), NSUB, IFACE, 1.0, 3.0, 0.5).astype(jnp.bfloat16)


def draw_local_inverse(key, part):
    return dominant_matrices(jax.random.fold_in(key, 2), NSUB, IFACE, 0.3, 1.0, 0.25).astype(jnp.bfloat16)


def draw_coarse_inverse(key, part):
    return dominant_matrices(jax.random.fold_in(key, 3), 1, NC, 1.0, 3.0, 0.5)[0].astype(jnp.bfloat16)


def draw_coarse_index(key, part):
    block_count = N_CROW * N_CCOL
    per_sub = MODES * SUB_DEV
    mean_count = per_sub // block_count
    block_width = NC // block_count
    split_keys = jax.random.split(jax.random.fold_in(key, 4), 3)
    pair_count = N_SUB // 2

    def choose_blocks(one_key):
        return jax.random.permutation(one_key, block_count)[:2]
    chosen = jax.vmap(choose_blocks)(jax.random.split(split_keys[0], pair_count))
    labels = jnp.arange(block_count, dtype=jnp.int32)[None, :]
    swing = (labels == chosen[:, 0:1]).astype(jnp.int32) - (labels == chosen[:, 1:2]).astype(jnp.int32)
    counts = mean_count + mean_count * jnp.stack([swing, -swing], axis=1).reshape(N_SUB, block_count)
    offsets = jnp.cumsum(counts, axis=0) - counts
    block_ends = jnp.cumsum(counts, axis=1)

    def shuffle_block(one_key):
        return jax.random.permutation(one_key, block_width)
    positions_perm = jax.vmap(shuffle_block)(jax.random.split(split_keys[1], block_count))
    slot_index = jnp.arange(per_sub, dtype=jnp.int32)
    block_of = jnp.sum((slot_index[None, :, None] >= block_ends[:, None, :]).astype(jnp.int32), axis=2)
    block_starts = jnp.take_along_axis(block_ends - counts, block_of, axis=1)
    within = slot_index[None, :] - block_starts
    position = jnp.take_along_axis(offsets, block_of, axis=1) + within
    values = block_of * block_width + positions_perm[block_of, position]

    def shuffle_rows(one_key):
        return jax.random.permutation(one_key, per_sub)
    shuffle_order = jax.vmap(shuffle_rows)(jax.random.split(split_keys[2], N_SUB))
    shuffled = jnp.take_along_axis(values, shuffle_order, axis=1)
    return shuffled.reshape(N_SUB * SUB_DEV, MODES).astype(jnp.int32)


def face_rows(key):
    face_key = jax.random.fold_in(key, 7)

    def shuffle_face(one_key):
        return jax.random.permutation(one_key, IFACE)
    orders = jax.vmap(shuffle_face)(jax.random.split(face_key, NSUB))
    return (orders[:, :FACE].astype(jnp.int32), orders[:, FACE:2 * FACE].astype(jnp.int32))


def draw_left_rows(key, part):
    return face_rows(key)[0]


def draw_right_rows(key, part):
    return face_rows(key)[1]


def levels(rng, dims, shards, smallest, largest):
    def one(axis_at, blocks):
        draws = jax.random.uniform(jax.random.fold_in(jax.random.fold_in(rng, 6), axis_at), (blocks,), jnp.float32, smallest / len(shards), largest / len(shards))
        return jnp.repeat(jnp.exp(draws), dims[axis_at] // blocks).reshape((-1,) + (1,) * (len(dims) - axis_at - 1))

    level = one(*shards[0])
    for cut in shards[1:]:
        level = level * one(*cut)
    return level


def noise(rng, dims, scale, most, cuts=(), kind=jnp.bfloat16):
    entries = jax.random.normal(rng, dims, jnp.float32) * scale
    if len(cuts) > 0:
        entries = levels(rng, dims, cuts, -0.22, 0.18) * entries
    return jnp.clip(entries, min=-most, max=most).astype(kind)


def setup_inputs(seed: int = 0) -> dict:
    keys = jax.random.split(jax.random.key(seed), 9)
    loads = noise(keys[0], (NSUB, IFACE, CASES), 1.0, 6.0, ((0, 64),))
    stiffness = draw_stiffness(jax.random.fold_in(keys[8], 71), 0)
    local_inverse = draw_local_inverse(jax.random.fold_in(keys[8], 71), 0)
    coarse_basis = noise(keys[3], (NSUB, IFACE, MODES), IFACE ** -0.5, 0.1875, ((0, 64), (1, 8)))
    coarse_inverse = draw_coarse_inverse(jax.random.fold_in(keys[8], 71), 0)
    coarse_index = draw_coarse_index(jax.random.fold_in(keys[8], 71), 0)
    left_rows = draw_left_rows(jax.random.fold_in(keys[8], 71), 0)
    right_rows = draw_right_rows(jax.random.fold_in(keys[8], 71), 0)
    return {"loads": loads, "stiffness": stiffness, "local_inverse": local_inverse, "coarse_basis": coarse_basis, "coarse_inverse": coarse_inverse, "coarse_index": coarse_index, "left_rows": left_rows, "right_rows": right_rows}


def batched_dot(left_side, right_side):
    def single(operands):
        return jnp.dot(operands[0], operands[1], preferred_element_type=jnp.float32)
    return lax.map(single, (left_side, right_side))


def apply_stiffness(stiffness, iterate, left_rows, right_rows):
    product = batched_dot(stiffness, iterate.astype(jnp.bfloat16))
    rounded = lax.optimization_barrier(product.astype(jnp.bfloat16)).astype(jnp.float32)
    sub_rows = jnp.arange(NSUB, dtype=jnp.int32)[:, None]
    right_values = rounded[sub_rows, right_rows]
    left_values = rounded[sub_rows, left_rows]
    from_before = jnp.roll(right_values, 1, axis=0)
    from_after = jnp.roll(left_values, -1, axis=0)
    assembled = rounded.at[sub_rows, left_rows].add(from_before)
    return assembled.at[sub_rows, right_rows].add(from_after)


def precondition(residual, local_inverse, coarse_basis, coarse_inverse, coarse_index):
    local_part = batched_dot(local_inverse, residual)
    basis_turned = jnp.swapaxes(coarse_basis, 1, 2)
    restricted = batched_dot(basis_turned, residual).astype(jnp.bfloat16)
    flat_index = coarse_index.reshape(-1).astype(jnp.int32)
    ordered = jnp.zeros((NC, CASES), jnp.bfloat16).at[flat_index].set(restricted.reshape(NC, CASES))
    coarse = jnp.dot(coarse_inverse, ordered, preferred_element_type=jnp.float32).astype(jnp.bfloat16)
    picked = coarse[flat_index].reshape(NSUB, MODES, CASES)
    return local_part + batched_dot(coarse_basis, picked)


def reference(loads, stiffness, local_inverse, coarse_basis, coarse_inverse, coarse_index, left_rows, right_rows):
    first_pass = precondition(loads, local_inverse, coarse_basis, coarse_inverse, coarse_index)
    residual = loads.astype(jnp.float32) - apply_stiffness(stiffness, first_pass, left_rows, right_rows)
    second_pass = first_pass + precondition(residual.astype(jnp.bfloat16), local_inverse, coarse_basis, coarse_inverse, coarse_index)
    final_residual = loads.astype(jnp.float32) - apply_stiffness(stiffness, second_pass, left_rows, right_rows)
    return second_pass, final_residual
```

```python
import jax
import jax.numpy as jnp
from jax import lax
from jax.experimental import pallas as pl
from jax.experimental.pallas import tpu as pltpu
from jax.sharding import PartitionSpec as P

MESH = pl.DeviceIdType.MESH
F32, BF16, I32 = jnp.float32, jnp.bfloat16, jnp.int32
GROUP = 8
PLANE = 64
SIDE = 8
CAP = 24
SLOT = 32
BLOCK = 768
OWN = 96
PART = 12
STEP = 16
STAGES = ("place", "a", "b", "c", "d", "e", "v", "z", "before", "after", "r")


def dot(a, b):
    return jnp.dot(a, b, preferred_element_type=F32)


def dot_nt(a, b):
    return lax.dot_general(a, b, (((1,), (1,)), ((), ())), preferred_element_type=F32)


def kernel(
    loads, stiff, linv, basis, cinv, index_row, left, right,
    out_u, out_r,
    place_buf, cinv_wide, cinv_perm, bp, bext, pick_face, put_face, pick_coarse,
    sa, ra, gb, sc, rc, gd, re, pk, vb, zb, fs, nb, rf, local, first,
    send_sem, recv_sem,
):
    sub = lax.axis_index("sub")
    crow = lax.axis_index("crow")
    ccol = lax.axis_index("ccol")
    g = crow * 2 + ccol
    sy, sz = sub // SIDE, lax.rem(sub, SIDE)

    def group_peer(k):
        t = lax.rem(g + k, GROUP)
        return t, {"sub": sub, "crow": t // 2, "ccol": lax.rem(t, 2)}

    def plane_peer(k):
        y = lax.rem(sy + k // SIDE, SIDE)
        z = lax.rem(sz + lax.rem(k, SIDE), SIDE)
        return {"sub": y * SIDE + z, "crow": crow, "ccol": ccol}

    def line_peer(k):
        return {"sub": lax.rem(sub + k, PLANE), "crow": crow, "ccol": ccol}

    def sem_of(stage, p):
        i = STAGES.index(stage) * 2 + p
        return send_sem.at[i], recv_sem.at[i]

    def start(src, dst, stage, p, device):
        s, r = sem_of(stage, p)
        pltpu.make_async_remote_copy(
            src_ref=src, dst_ref=dst, send_sem=s, recv_sem=r, device_id=device, device_id_type=MESH
        ).start()

    def wait(ref, sem):
        pltpu.make_async_copy(ref, ref, sem).wait()

    def to_group(ref_of, dst, stage, p):
        def step(k, carry):
            t, device = group_peer(k)
            start(ref_of(t), dst, stage, p, device)
            return carry

        lax.fori_loop(1, GROUP, step, 0)

    def to_plane(ref, stage, p):
        def step(k, carry):
            start(ref, ref, stage, p, plane_peer(k))
            return carry

        lax.fori_loop(1, PLANE, step, 0)

    mine = pl.ds(pl.multiple_of(g * 128, 128), 128)

    for p in range(2):
        gb[p] = jnp.zeros(gb.shape[1:], BF16)
    pk[...] = jnp.zeros(pk.shape, BF16)

    barrier = pltpu.get_barrier_semaphore()

    def greet_group(k, carry):
        pl.semaphore_signal(barrier, inc=1, device_id=group_peer(k)[1], device_id_type=MESH)
        return carry

    def greet_plane(k, carry):
        pl.semaphore_signal(barrier, inc=1, device_id=plane_peer(k), device_id_type=MESH)
        return carry

    lax.fori_loop(1, GROUP, greet_group, 0)
    lax.fori_loop(1, PLANE, greet_plane, 0)

    lane = lax.broadcasted_iota(I32, (128, 128), 1).astype(F32)
    down = lax.broadcasted_iota(I32, (128, 128), 0).astype(F32)
    g_f = g.astype(F32)

    index_lane = jnp.broadcast_to(index_row[...].astype(F32), (128, 128))
    index_down = jnp.transpose(index_lane)

    def block_of(index):
        block = jnp.zeros(index.shape, F32)
        for t in range(1, GROUP):
            block += (index >= t * BLOCK).astype(F32)
        return jnp.where(index < 0, 99.0, block)

    block_lane, block_down = block_of(index_lane), block_of(index_down)
    earlier = (block_lane == block_down) & (down < lane)
    rank = jnp.sum(earlier.astype(F32), axis=0, keepdims=True)
    code_lane = jnp.broadcast_to(block_lane[0:1] * SLOT + rank, (128, 128))
    code_down = jnp.transpose(code_lane)
    select = jnp.concatenate(
        [(code_lane == down).astype(F32), (code_lane == down + 128.0).astype(F32)], axis=0
    ).astype(BF16)
    for s in range(2):
        k48 = lax.broadcasted_iota(I32, (48, 128), 0)
        l48 = lax.broadcasted_iota(I32, (48, 128), 1)
        shift = (l48 == k48 + 48 * s).astype(F32).astype(BF16)
        bext[s] = dot(basis[s], shift).astype(BF16)
        bp[s] = dot_nt(select, bext[s]).astype(BF16)

    slot = lane - SLOT * lax.rem(sub, 4).astype(F32)
    hit = (code_down == g_f * SLOT + slot) & (slot >= 0) & (slot < SLOT)
    place = jnp.sum(jnp.where(hit, index_down - g_f * BLOCK + 1.0, 0.0), axis=0, keepdims=True)
    place_buf[sub] = place

    def restrict(rows):
        part = dot(bp[0], rows[0]) + dot(bp[1], rows[1])
        return part.reshape(GROUP, SLOT, 128)

    sa[0] = restrict([loads[s, mine] for s in range(2)])

    pl.semaphore_wait(barrier, GROUP + PLANE - 2)

    def exchange_restricted(p):
        ra[p, g] = sa[p, g]
        to_group(
            lambda t: sa.at[p, t, pl.ds(0, CAP)], ra.at[p, g, pl.ds(0, CAP)], "a", p
        )

    def spread_restricted(p):
        wait(ra.at[p, pl.ds(0, GROUP - 1), pl.ds(0, CAP)], sem_of("a", p)[1])
        total = ra[p, 0, 0:CAP]
        for t in range(1, GROUP):
            total += ra[p, t, 0:CAP]
        gb[p, sub, 0:CAP] = total.astype(BF16)
        to_plane(gb.at[p, sub, pl.ds(0, CAP)], "b", p)

    exchange_restricted(0)
    to_plane(place_buf.at[sub], "place", 0)

    for s in range(2):
        local[s] = dot(linv[s], loads[s])
    spread_restricted(0)

    wide = (
        lax.broadcasted_iota(I32, (128, OWN), 1)
        == (lax.broadcasted_iota(I32, (128, OWN), 0) // STEP) * PART
        + lax.rem(lax.broadcasted_iota(I32, (128, OWN), 0), STEP)
    ) & (lax.rem(lax.broadcasted_iota(I32, (128, OWN), 0), STEP) < PART)
    cinv_wide[...] = dot(wide.astype(F32).astype(BF16), cinv[...]).astype(BF16)

    for s in range(2):
        for side, rows in enumerate((left, right)):
            row_lane = jnp.broadcast_to(rows[s : s + 1, :].astype(F32), (128, 128))
            row_down = jnp.transpose(row_lane)
            for j in range(8):
                pick_face[s, side, :, j * 128 : (j + 1) * 128] = (
                    (row_down == lane + 128.0 * j).astype(F32).astype(BF16)
                )
            put_face[s, side] = (row_lane == down + 128.0 * g_f).astype(F32).astype(BF16)
    for j in range(8):
        column = lax.broadcasted_iota(I32, (128, 128), 1) + 128 * j
        within = lax.rem(column, STEP)
        row_of = jnp.where(within < PART, (column // STEP) * OWN + PART * g + within, -5)
        pick_coarse[:, j * 128 : (j + 1) * 128] = (
            (index_down == row_of.astype(F32)).astype(F32).astype(BF16)
        )

    wait(place_buf.at[pl.ds(0, PLANE - 1)], sem_of("place", 0)[1])
    tall = lax.broadcasted_iota(I32, (BLOCK, 128), 0).astype(F32) + 1.0

    def permute(c, carry):
        spot = (
            place_buf[4 * c] + place_buf[4 * c + 1] + place_buf[4 * c + 2] + place_buf[4 * c + 3]
        )
        chosen = (tall == spot).astype(F32).astype(BF16)
        cinv_perm[:, pl.ds(pl.multiple_of(c * 128, 128), 128)] = dot(
            cinv_wide[...], chosen
        ).astype(BF16)
        return carry

    lax.fori_loop(0, PLANE // 4, permute, 0)

    def coarse(p):
        wait(gb.at[p, pl.ds(0, PLANE - 1), pl.ds(0, CAP)], sem_of("b", p)[1])
        part = dot(cinv_perm[...], gb[p].reshape(PLANE * SLOT, 128))
        sc[p] = part.reshape(GROUP, STEP, 128)
        rc[p, g] = sc[p, g]
        to_group(lambda t: sc.at[p, t], rc.at[p, g], "c", p)
        wait(rc.at[p, pl.ds(0, GROUP - 1)], sem_of("c", p)[1])
        total = rc[p, 0]
        for t in range(1, GROUP):
            total += rc[p, t]
        gd[p, sub] = total.astype(BF16)
        to_plane(gd.at[p, sub], "d", p)
        wait(gd.at[p, pl.ds(0, PLANE - 1)], sem_of("d", p)[1])
        found = dot(pick_coarse[...], gd[p].reshape(PLANE * STEP, 128))
        re[p, g] = found[0:OWN].astype(BF16)
        to_group(lambda t: re.at[p, g], re.at[p, g], "e", p)
        wait(re.at[p, pl.ds(0, GROUP - 1)], sem_of("e", p)[1])
        picked = re[p, 0].astype(F32)
        for t in range(1, GROUP):
            picked += re[p, t].astype(F32)
        pk[p, 0:OWN] = picked.astype(BF16)
        return [dot(bext[s], pk[p]) for s in range(2)]

    def apply(p, iterate):
        for s in range(2):
            vb[p, s, mine] = iterate[s].astype(BF16)
        to_group(lambda t: vb.at[p, :, mine], vb.at[p, :, mine], "v", p)
        wait(vb.at[p, :, pl.ds(0, 896)], sem_of("v", p)[1])
        image = []
        for s in range(2):
            z = dot(stiff[s], vb[p, s]).astype(BF16)
            zb[p, s, mine] = z
            image.append(z.astype(F32))
        to_group(lambda t: zb.at[p, :, mine], zb.at[p, :, mine], "z", p)
        wait(zb.at[p, :, pl.ds(0, 896)], sem_of("z", p)[1])
        fs[p, 0] = dot(pick_face[0, 0], zb[p, 0]).astype(BF16)
        fs[p, 1] = dot(pick_face[1, 1], zb[p, 1]).astype(BF16)
        start(fs.at[p, 0], nb.at[p, 1], "after", p, line_peer(PLANE - 1))
        start(fs.at[p, 1], nb.at[p, 0], "before", p, line_peer(1))
        to_one = dot(pick_face[0, 1], zb[p, 0]).astype(BF16)
        to_zero = dot(pick_face[1, 0], zb[p, 1]).astype(BF16)
        image[0] = image[0] + dot(put_face[0, 1], to_zero)
        image[1] = image[1] + dot(put_face[1, 0], to_one)
        wait(nb.at[p, 0], sem_of("before", p)[1])
        wait(nb.at[p, 1], sem_of("after", p)[1])
        image[0] = image[0] + dot(put_face[0, 0], nb[p, 0])
        image[1] = image[1] + dot(put_face[1, 1], nb[p, 1])
        return [loads[s, mine].astype(F32) - image[s] for s in range(2)]

    correction = coarse(0)
    for s in range(2):
        first[s] = local[s] + correction[s]
    residual = apply(0, [first[s] for s in range(2)])

    for s in range(2):
        rf[s, mine] = residual[s].astype(BF16)
    sa[1] = restrict([rf[s, mine] for s in range(2)])
    exchange_restricted(1)
    to_group(lambda t: rf.at[:, mine], rf.at[:, mine], "r", 0)
    spread_restricted(1)
    wait(rf.at[:, pl.ds(0, 896)], sem_of("r", 0)[1])
    for s in range(2):
        local[s] = dot(linv[s], rf[s])
    correction = coarse(1)
    for s in range(2):
        out_u[s] = first[s] + (local[s] + correction[s])
    final = apply(1, [out_u[s] for s in range(2)])
    for s in range(2):
        out_r[s] = final[s]

    wait(place_buf.at[pl.ds(0, PLANE - 1)], sem_of("place", 0)[0])
    wait(rf.at[:, pl.ds(0, 896)], sem_of("r", 0)[0])
    for p in range(2):
        wait(ra.at[p, pl.ds(0, GROUP - 1), pl.ds(0, CAP)], sem_of("a", p)[0])
        wait(gb.at[p, pl.ds(0, PLANE - 1), pl.ds(0, CAP)], sem_of("b", p)[0])
        wait(rc.at[p, pl.ds(0, GROUP - 1)], sem_of("c", p)[0])
        wait(gd.at[p, pl.ds(0, PLANE - 1)], sem_of("d", p)[0])
        wait(re.at[p, pl.ds(0, GROUP - 1)], sem_of("e", p)[0])
        wait(vb.at[p, :, pl.ds(0, 896)], sem_of("v", p)[0])
        wait(zb.at[p, :, pl.ds(0, 896)], sem_of("z", p)[0])
        wait(nb.at[p, 0], sem_of("before", p)[0])
        wait(nb.at[p, 1], sem_of("after", p)[0])


def body(loads, stiffness, local_inverse, coarse_basis, coarse_inverse, coarse_index, left, right):
    index_row = jnp.pad(coarse_index.reshape(1, OWN), ((0, 0), (0, 128 - OWN)), constant_values=-1)
    vmem = pl.BlockSpec(memory_space=pltpu.VMEM)
    out = jax.ShapeDtypeStruct((2, 128, 128), F32)
    count = 2 * len(STAGES)
    return pl.pallas_call(
        kernel,
        out_shape=(out, out),
        in_specs=[vmem] * 8,
        out_specs=(vmem, vmem),
        scratch_shapes=[
            pltpu.VMEM((PLANE, 1, 128), F32),
            pltpu.VMEM((128, BLOCK), BF16),
            pltpu.VMEM((128, PLANE * SLOT), BF16),
            pltpu.VMEM((2, GROUP * SLOT, 128), BF16),
            pltpu.VMEM((2, 128, 128), BF16),
            pltpu.VMEM((2, 2, 128, 1024), BF16),
            pltpu.VMEM((2, 2, 128, 128), BF16),
            pltpu.VMEM((128, PLANE * STEP), BF16),
            pltpu.VMEM((2, GROUP, SLOT, 128), F32),
            pltpu.VMEM((2, GROUP, SLOT, 128), F32),
            pltpu.VMEM((2, PLANE, SLOT, 128), BF16),
            pltpu.VMEM((2, GROUP, STEP, 128), F32),
            pltpu.VMEM((2, GROUP, STEP, 128), F32),
            pltpu.VMEM((2, PLANE, STEP, 128), BF16),
            pltpu.VMEM((2, GROUP, OWN, 128), BF16),
            pltpu.VMEM((2, 128, 128), BF16),
            pltpu.VMEM((2, 2, 1024, 128), BF16),
            pltpu.VMEM((2, 2, 1024, 128), BF16),
            pltpu.VMEM((2, 2, 128, 128), BF16),
            pltpu.VMEM((2, 2, 128, 128), BF16),
            pltpu.VMEM((2, 1024, 128), BF16),
            pltpu.VMEM((2, 128, 128), F32),
            pltpu.VMEM((2, 128, 128), F32),
            pltpu.SemaphoreType.DMA((count,)),
            pltpu.SemaphoreType.DMA((count,)),
        ],
        compiler_params=pltpu.CompilerParams(collective_id=0, has_side_effects=True),
        name="schwarz",
    )(loads, stiffness, local_inverse, coarse_basis, coarse_inverse, index_row, left, right)


def solution(mesh):
    group = ("crow", "ccol")
    return jax.shard_map(
        body,
        mesh=mesh,
        in_specs=(
            P("sub", None, None),
            P("sub", group, None),
            P("sub", group, None),
            P("sub", group, None),
            P("sub", group),
            P("sub", None),
            P("sub", None),
            P("sub", None),
        ),
        out_specs=(P("sub", group, None), P("sub", group, None)),
        check_vma=False,
    )
```

```python
import jax
import jax.numpy as jnp
from jax import lax
from jax.experimental import pallas as pl
from jax.experimental.pallas import tpu as pltpu
from jax.sharding import PartitionSpec as P

MESH = pl.DeviceIdType.MESH
F32, BF16, I32 = jnp.float32, jnp.bfloat16, jnp.int32
GROUP = 8
PLANE = 64
SIDE = 8
CAP = 24
HEAD, TAIL = 16, 8
BLOCK = 768
OWN = 96
MODES = 48
STEP = 16
STAGES = ("basis", "faces", "a", "c", "d", "e", "w", "r", "inner", "before", "after")
PIPES = ("place", "b0", "b1")
NEAREST = (1, 7, 2, 6, 3, 5, 4)


def dot(a, b):
    return jnp.dot(a, b, preferred_element_type=F32)


def dot_tn(a, b):
    return lax.dot_general(a, b, (((0,), (0,)), ((), ())), preferred_element_type=F32)


def mask(condition):
    return condition.astype(F32).astype(BF16)


def iota(shape, dim):
    return lax.broadcasted_iota(I32, shape, dim)


def kernel(
    loads_in, stiff_in, linv_in, basis, cinv_in, index_in, left, right,
    out_u, out_r,
    loads, stiff, linv, cinv,
    place_buf, cinv_wide, perm_head, perm_tail, bp, basis_t, basis_full, put_face, pick_coarse,
    face_part, face_got, face_own, sa, ra, head, tail, sc, rc, gd, re, pk, wb, vb, fs, nb, rf, local, first, restricted,
    send_sem, recv_sem, near_recv, far_recv, near_send, far_send, load_sem,
):
    sub = lax.axis_index("sub")
    crow = lax.axis_index("crow")
    ccol = lax.axis_index("ccol")
    core = lax.rem(crow, 2)
    chip = (crow // 2) * 2 + ccol
    g = crow * 2 + ccol
    sy, sz = sub // SIDE, lax.rem(sub, SIDE)
    q1 = sz * (1 - core) + sy * core
    q2 = sy * (1 - core) + sz * core

    def group_peer(k):
        t = lax.rem(g + k, GROUP)
        return t, {"sub": sub, "crow": t // 2, "ccol": lax.rem(t, 2)}

    def plane_at(a, b):
        y = b * (1 - core) + a * core
        z = a * (1 - core) + b * core
        return {"sub": y * SIDE + z, "crow": crow, "ccol": ccol}

    def first_peer(d):
        return plane_at(lax.rem(q1 + d, SIDE), q2)

    def second_peer(d):
        return plane_at(q1, lax.rem(q2 + d, SIDE))

    def plane_peer(k):
        y = lax.rem(sy + k // SIDE, SIDE)
        z = lax.rem(sz + lax.rem(k, SIDE), SIDE)
        return {"sub": y * SIDE + z, "crow": crow, "ccol": ccol}

    def copy(src, dst, s, r, device):
        pltpu.make_async_remote_copy(
            src_ref=src, dst_ref=dst, send_sem=s, recv_sem=r, device_id=device, device_id_type=MESH
        ).start()

    def wait(ref, sem):
        pltpu.make_async_copy(ref, ref, sem).wait()

    def repeat(low, high, step):
        def one(k, carry):
            step(k)
            return carry

        lax.fori_loop(low, high, one, 0)

    def sems(stage, p):
        i = STAGES.index(stage) * 2 + p
        return send_sem.at[i], recv_sem.at[i]

    def to_group(ref_of, dst, stage, p):
        s, r = sems(stage, p)

        def step(k):
            t, device = group_peer(k)
            copy(ref_of(t), dst, s, r, device)

        repeat(1, GROUP, step)

    mine = pl.ds(pl.multiple_of(g * 128, 128), 128)
    seven = pl.ds(0, 7)

    arrivals = {
        "basis": lambda p: basis_t.at[:, pl.ds(0, 896)],
        "faces": lambda p: face_got.at[seven],
        "a": lambda p: ra.at[seven],
        "c": lambda p: rc.at[p, seven],
        "e": lambda p: re.at[p, seven],
        "w": lambda p: wb.at[p, :, pl.ds(0, 896)],
        "r": lambda p: rf.at[:, pl.ds(0, 896)],
        "inner": lambda p: nb.at[p, pl.ds(0, 2), seven],
        "before": lambda p: nb.at[p, 2],
        "after": lambda p: nb.at[p, 3],
    }

    def arrived(stage, p):
        wait(arrivals[stage](p), sems(stage, p)[1])

    def spot(half):
        return (q2, q1) if half == 0 else (q1, q2)

    def near_peer(half, d):
        return first_peer(d) if half == 0 else second_peer(d)

    def far_peer(half, d):
        return second_peer(d) if half == 0 else first_peer(d)

    def pipe_start(name, refs):
        i = PIPES.index(name)

        def near(d):
            for half, ref in enumerate(refs):
                block = ref.at[spot(half)]
                copy(block, block, near_send.at[i, half], near_recv.at[i, half, d], near_peer(half, d))

        def far(d):
            for half, ref in enumerate(refs):
                block = ref.at[spot(half)]
                copy(block, block, far_send.at[i, half], far_recv.at[i, half], far_peer(half, d))

        repeat(1, SIDE, near)
        repeat(1, SIDE, far)

    def pipe_forward(name, refs):
        i = PIPES.index(name)
        for e in NEAREST:
            for half, ref in enumerate(refs):
                a, b = spot(half)
                block = ref.at[a, lax.rem(b + SIDE - e, SIDE)]
                wait(block, near_recv.at[i, half, e])

                def far(d):
                    copy(block, block, far_send.at[i, half], far_recv.at[i, half], far_peer(half, d))

                repeat(1, SIDE, far)

    def pipe_wait(name, refs):
        i = PIPES.index(name)
        for half, ref in enumerate(refs):
            wait(ref.at[seven], far_recv.at[i, half])

    def pipe_settle(name, refs):
        i = PIPES.index(name)
        for half, ref in enumerate(refs):
            wait(ref.at[0, seven], near_send.at[i, half])
            wait(ref.at[seven], far_send.at[i, half])

    gd[...] = jnp.zeros(gd.shape, BF16)
    pk[...] = jnp.zeros(pk.shape, BF16)

    barrier = pltpu.get_barrier_semaphore()

    def greet(k):
        for device in (group_peer(k)[1], first_peer(k), second_peer(k)):
            pl.semaphore_signal(barrier, inc=1, device_id=device, device_id_type=MESH)

    repeat(1, SIDE, greet)

    operands = ((stiff_in, stiff), (linv_in, linv), (loads_in, loads), (cinv_in, cinv))
    for i, (outer, inner) in enumerate(operands):
        pltpu.make_async_copy(outer, inner, load_sem.at[i]).start()

    lane_i, down_i = iota((128, 128), 1), iota((128, 128), 0)
    lane, down = lane_i.astype(F32), down_i.astype(F32)
    g_f = g.astype(F32)

    index_lane = jnp.zeros((8, 128), F32)
    for s in range(2):
        shift = mask(iota((MODES, 128), 1) == iota((MODES, 128), 0) + MODES * s)
        index = jnp.broadcast_to(index_in[s : s + 1, :], (8, MODES))
        high = lax.shift_right_logical(index, 6)
        low = index - high * 64
        index_lane += 64.0 * dot(high.astype(F32).astype(BF16), shift)
        index_lane += dot(low.astype(F32).astype(BF16), shift)
    index_lane = jnp.broadcast_to(index_lane[0:1], (128, 128))
    index_lane = jnp.where(lane < OWN, index_lane, -1.0)
    index_down = jnp.transpose(index_lane)

    def block_of(index):
        block = jnp.zeros(index.shape, F32)
        for t in range(1, GROUP):
            block += (index >= t * BLOCK).astype(F32)
        return jnp.where(index < 0, 99.0, block)

    block_lane, block_down = block_of(index_lane), block_of(index_down)
    earlier = (block_lane == block_down) & (down < lane)
    rank = jnp.sum(earlier.astype(F32), axis=0, keepdims=True)
    code_lane = jnp.broadcast_to(block_lane[0:1] * CAP + rank, (128, 128))
    code_down = jnp.transpose(code_lane)
    select_own = mask(code_lane[0:CAP] == down[0:CAP] + g_f * CAP)

    slot = lane - (q1 * HEAD).astype(F32)
    in_head = (code_down == g_f * CAP + slot) & (slot >= 0) & (slot < HEAD)
    slot = lane - (lax.rem(q1, 2) * 64 + q2 * TAIL).astype(F32)
    in_tail = (code_down == g_f * CAP + HEAD + slot) & (slot >= 0) & (slot < TAIL)
    value = index_down - g_f * BLOCK + 1.0
    place_buf[q2, q1, :, 0:128] = jnp.sum(jnp.where(in_head, value, 0.0), axis=0, keepdims=True)
    place_buf[q2, q1, :, 128:256] = jnp.sum(jnp.where(in_tail, value, 0.0), axis=0, keepdims=True)

    basis_own = basis[...].reshape(OWN, 128)
    basis_t[:, mine] = basis_own

    pl.semaphore_wait(barrier, GROUP + 2 * SIDE - 3)

    to_group(lambda t: basis_t.at[:, mine], basis_t.at[:, mine], "basis", 0)
    pipe_start("place", [place_buf])

    for i, (outer, inner) in enumerate(operands):
        pltpu.make_async_copy(outer, inner, load_sem.at[i]).wait()
    for s in range(2):
        for side, rows in enumerate((left, right)):
            row_lane = jnp.broadcast_to(rows[s : s + 1, :].astype(F32), (128, 128))
            put = row_lane == down + 128.0 * g_f
            put_face[s, side] = mask(put)
            pick = mask(jnp.transpose(put.astype(F32)) > 0.5)
            part = dot(pick, stiff[s]).astype(BF16)
            face_part[:, (2 * s + side) * STEP : (2 * s + side + 1) * STEP, :] = part.reshape(
                GROUP, STEP, 1024
            )

    def settle_faces():
        total = face_got[0]
        for t in range(1, GROUP):
            total += face_got[t]
        face_own[...] = total

    arrived("basis", 0)
    for s in range(2):
        restricted[s * MODES : (s + 1) * MODES] = dot(
            basis_t[s * MODES : (s + 1) * MODES, :], loads[s]
        ).astype(BF16)
    rows = dot(select_own[:, 0:OWN], restricted[...]).astype(BF16)

    def spread(p, rows):
        head[(p, *spot(0))] = rows[0:HEAD]
        tail[(p, *spot(1))] = rows[HEAD:CAP]
        pipe_start(PIPES[1 + p], [head.at[p], tail.at[p]])

    spread(0, rows)
    face_got[g] = face_part[g]
    to_group(lambda t: face_part.at[t], face_got.at[g], "faces", 0)
    pipe_forward("place", [place_buf])
    pipe_forward("b0", [head.at[0], tail.at[0]])

    out_row, out_of = iota((128, OWN), 0), iota((128, OWN), 1)
    part_of, within = out_row // STEP, lax.rem(out_row, STEP)
    part_core = lax.rem(part_of // 2, 2)
    part_chip = (part_of // 4) * 2 + lax.rem(part_of, 2)
    wide = (out_of == part_chip * CAP + part_core * STEP + within) & (within < STEP - 8 * part_core)
    cinv_wide[...] = dot(mask(wide), cinv[...]).astype(BF16)
    for j in range(8):
        column = lane_i + 128 * j
        within = lax.rem(column, STEP)
        row_of = (column // STEP) * OWN + chip * CAP + core * STEP + within
        row_of = jnp.where(within < STEP - 8 * core, row_of, -5)
        pick_coarse[:, j * 128 : (j + 1) * 128] = mask(index_down == row_of.astype(F32))[0:OWN]
    for s in range(2):
        for j in range(8):
            shift = mask(iota((MODES, 128), 1) == iota((MODES, 128), 0) + MODES * s)
            turned = dot_tn(basis_t[s * MODES : (s + 1) * MODES, j * 128 : (j + 1) * 128], shift)
            basis_full[s, j * 128 : (j + 1) * 128, :] = turned.astype(BF16)
    select = mask(
        jnp.broadcast_to(code_lane[0:1], (GROUP * CAP, 128)) == iota((GROUP * CAP, 128), 0).astype(F32)
    )
    for s in range(2):
        keep = (iota((OWN, 128), 0) >= s * MODES) & (iota((OWN, 128), 0) < (s + 1) * MODES)
        part = jnp.where(keep, basis_own.astype(F32), 0.0).astype(BF16)
        bp[s] = dot(select[:, 0:OWN], part).astype(BF16)

    pipe_wait("place", [place_buf])
    tall = iota((BLOCK, 128), 0).astype(F32) + 1.0
    for c in range(8):
        where = jnp.sum(place_buf[c, :, 0, 0:128], axis=0, keepdims=True)
        perm_head[:, c * 128 : (c + 1) * 128] = dot(cinv_wide[...], mask(tall == where)).astype(BF16)
    for c in range(4):
        where = jnp.sum(
            place_buf[:, 2 * c, 0, 128:256] + place_buf[:, 2 * c + 1, 0, 128:256], axis=0, keepdims=True
        )
        perm_tail[:, c * 128 : (c + 1) * 128] = dot(cinv_wide[...], mask(tall == where)).astype(BF16)
    for s in range(2):
        local[s] = dot(linv[s], loads[s])
        wb[0, s, mine] = local[s].astype(BF16)

    def coarse_start(p):
        pipe_wait(PIPES[1 + p], [head.at[p], tail.at[p]])
        part = dot(perm_head[...], head[p].reshape(PLANE * HEAD, 128))
        part += dot(perm_tail[...], tail[p].reshape(PLANE * TAIL, 128))
        sc[p] = part.reshape(GROUP, STEP, 128)
        rc[p, g] = sc[p, g]
        to_group(lambda t: sc.at[p, t], rc.at[p, g], "c", p)
        arrived("c", p)
        total = rc[p, 0]
        for t in range(1, GROUP):
            total += rc[p, t]
        gd[p, sub] = total.astype(BF16)
        s, r = sems("d", p)
        for kind, size in enumerate((16, 8)):
            @pl.when(core == kind)
            def _():
                block = gd.at[p, sub, pl.ds(0, size)]
                repeat(1, PLANE, lambda k: copy(block, block, s, r, plane_peer(k)))

    def each_plane(p, which):
        for kind, size in enumerate((16, 8)):
            @pl.when(core == kind)
            def _():
                wait(gd.at[p, pl.ds(0, PLANE - 1), pl.ds(0, size)], sems("d", p)[which])

    def coarse_end(p):
        each_plane(p, 1)
        found = dot(pick_coarse[...], gd[p].reshape(PLANE * STEP, 128))
        re[p, g] = found.astype(BF16)
        to_group(lambda t: re.at[p, g], re.at[p, g], "e", p)
        arrived("e", p)
        picked = re[p, 0].astype(F32)
        for t in range(1, GROUP):
            picked += re[p, t].astype(F32)
        pk[p, 0:OWN] = picked.astype(BF16)

    def apply(p):
        arrived("w", p)
        for s in range(2):
            vb[s] = (wb[p, s].astype(F32) + dot(basis_full[s], pk[p])).astype(BF16)
        faces = [dot(face_own[2 * STEP * s : 2 * STEP * (s + 1)], vb[s]).astype(BF16) for s in range(2)]
        nb[p, 0, g] = faces[1][0:STEP]
        nb[p, 1, g] = faces[0][STEP : 2 * STEP]
        fs[p, 0] = faces[0][0:STEP]
        fs[p, 1] = faces[1][STEP : 2 * STEP]
        s_before, r_before = sems("before", p)
        s_after, r_after = sems("after", p)

        def outward(k):
            t = lax.rem(g + k, GROUP)
            place = {"crow": t // 2, "ccol": lax.rem(t, 2)}
            up = {"sub": lax.rem(sub + 1, PLANE), **place}
            low = {"sub": lax.rem(sub + PLANE - 1, PLANE), **place}
            copy(fs.at[p, 1], nb.at[p, 2, g], s_before, r_before, up)
            copy(fs.at[p, 0], nb.at[p, 3, g], s_after, r_after, low)

        repeat(0, GROUP, outward)
        inner = nb.at[p, pl.ds(0, 2), g]
        to_group(lambda t: inner, inner, "inner", p)
        image = [dot(stiff[s], vb[s]).astype(BF16).astype(F32) for s in range(2)]
        arrived("inner", p)
        image[0] += dot(put_face[0, 1], nb[p, 0].reshape(128, 128))
        image[1] += dot(put_face[1, 0], nb[p, 1].reshape(128, 128))
        arrived("before", p)
        image[0] += dot(put_face[0, 0], nb[p, 2].reshape(128, 128))
        arrived("after", p)
        image[1] += dot(put_face[1, 1], nb[p, 3].reshape(128, 128))
        return [loads[s, mine].astype(F32) - image[s] for s in range(2)]

    coarse_start(0)
    to_group(lambda t: wb.at[0, :, mine], wb.at[0, :, mine], "w", 0)
    arrived("faces", 0)
    settle_faces()
    coarse_end(0)
    for s in range(2):
        first[s] = local[s] + dot(basis_full[s, mine], pk[0])
    residual = apply(0)

    for s in range(2):
        rf[s, mine] = residual[s].astype(BF16)
    part = dot(bp[0], rf[0, mine]) + dot(bp[1], rf[1, mine])
    sa[...] = part.reshape(GROUP, CAP, 128)
    ra[g] = sa[g]
    to_group(lambda t: sa.at[t], ra.at[g], "a", 0)
    arrived("a", 0)
    total = ra[0]
    for t in range(1, GROUP):
        total += ra[t]
    spread(1, total.astype(BF16))
    to_group(lambda t: rf.at[:, mine], rf.at[:, mine], "r", 0)
    pipe_forward("b1", [head.at[1], tail.at[1]])
    arrived("r", 0)
    for s in range(2):
        local[s] = dot(linv[s], rf[s])
        wb[1, s, mine] = (first[s] + local[s]).astype(BF16)
    coarse_start(1)
    to_group(lambda t: wb.at[1, :, mine], wb.at[1, :, mine], "w", 1)
    coarse_end(1)
    for s in range(2):
        out_u[s] = first[s] + (local[s] + dot(basis_full[s, mine], pk[1]))
    final = apply(1)
    for s in range(2):
        out_r[s] = final[s]

    for stage in ("basis", "faces", "a", "r"):
        wait(arrivals[stage](0), sems(stage, 0)[0])
    pipe_settle("place", [place_buf])
    for p in range(2):
        for stage in ("c", "e", "w", "inner", "before", "after"):
            wait(arrivals[stage](p), sems(stage, p)[0])
        each_plane(p, 0)
        pipe_settle(PIPES[1 + p], [head.at[p], tail.at[p]])


def body(loads, stiffness, local_inverse, coarse_basis, coarse_inverse, coarse_index, left, right):
    vmem = pl.BlockSpec(memory_space=pltpu.VMEM)
    away = pl.BlockSpec(memory_space=pl.ANY)
    out = jax.ShapeDtypeStruct((2, 128, 128), F32)
    count = 2 * len(STAGES)
    dma = pltpu.SemaphoreType.DMA
    return pl.pallas_call(
        kernel,
        out_shape=(out, out),
        in_specs=[away, away, away, vmem, away, vmem, vmem, vmem],
        out_specs=(vmem, vmem),
        scratch_shapes=[
            pltpu.VMEM((2, 1024, 128), BF16),
            pltpu.VMEM((2, 128, 1024), BF16),
            pltpu.VMEM((2, 128, 1024), BF16),
            pltpu.VMEM((OWN, BLOCK), BF16),
            pltpu.VMEM((SIDE, SIDE, 1, 256), F32),
            pltpu.VMEM((128, BLOCK), BF16),
            pltpu.VMEM((128, PLANE * HEAD), BF16),
            pltpu.VMEM((128, PLANE * TAIL), BF16),
            pltpu.VMEM((2, GROUP * CAP, 128), BF16),
            pltpu.VMEM((OWN, 1024), BF16),
            pltpu.VMEM((2, 1024, 128), BF16),
            pltpu.VMEM((2, 2, 128, 128), BF16),
            pltpu.VMEM((OWN, PLANE * STEP), BF16),
            pltpu.VMEM((GROUP, 4 * STEP, 1024), BF16),
            pltpu.VMEM((GROUP, 4 * STEP, 1024), BF16),
            pltpu.VMEM((4 * STEP, 1024), BF16),
            pltpu.VMEM((GROUP, CAP, 128), F32),
            pltpu.VMEM((GROUP, CAP, 128), F32),
            pltpu.VMEM((2, SIDE, SIDE, HEAD, 128), BF16),
            pltpu.VMEM((2, SIDE, SIDE, TAIL, 128), BF16),
            pltpu.VMEM((2, GROUP, STEP, 128), F32),
            pltpu.VMEM((2, GROUP, STEP, 128), F32),
            pltpu.VMEM((2, PLANE, STEP, 128), BF16),
            pltpu.VMEM((2, GROUP, OWN, 128), BF16),
            pltpu.VMEM((2, 128, 128), BF16),
            pltpu.VMEM((2, 2, 1024, 128), BF16),
            pltpu.VMEM((2, 1024, 128), BF16),
            pltpu.VMEM((2, 2, STEP, 128), BF16),
            pltpu.VMEM((2, 4, GROUP, STEP, 128), BF16),
            pltpu.VMEM((2, 1024, 128), BF16),
            pltpu.VMEM((2, 128, 128), F32),
            pltpu.VMEM((2, 128, 128), F32),
            pltpu.VMEM((OWN, 128), BF16),
            dma((count,)),
            dma((count,)),
            dma((len(PIPES), 2, SIDE)),
            dma((len(PIPES), 2)),
            dma((len(PIPES), 2)),
            dma((len(PIPES), 2)),
            dma((4,)),
        ],
        compiler_params=pltpu.CompilerParams(collective_id=0, has_side_effects=True),
        name="schwarz",
    )(
        loads, stiffness, local_inverse, jnp.swapaxes(coarse_basis, 1, 2), coarse_inverse, coarse_index, left, right
    )


def solution(mesh):
    group = ("crow", "ccol")
    return jax.shard_map(
        body,
        mesh=mesh,
        in_specs=(
            P("sub", None, None),
            P("sub", group, None),
            P("sub", group, None),
            P("sub", group, None),
            P("sub", group),
            P("sub", None),
            P("sub", None),
            P("sub", None),
        ),
        out_specs=(P("sub", group, None), P("sub", group, None)),
        check_vma=False,
    )
```

```python
import jax
import jax.numpy as jnp
from jax import lax
from jax.experimental import pallas as pl
from jax.experimental.pallas import tpu as pltpu
from jax.sharding import PartitionSpec as P

MESH = pl.DeviceIdType.MESH
F32, BF16, I32 = jnp.float32, jnp.bfloat16, jnp.int32
GROUP = 8
PLANE = 64
SIDE = 8
CAP = 24
HEAD, TAIL = 16, 8
BLOCK = 768
OWN = 96
MODES = 48
STEP = 16
STAGES = ("basis", "faces", "a", "c", "d", "e", "w", "r", "inner", "before", "after")
PIPES = ("place", "b0", "b1")
NEAREST = (1, 7, 2, 6, 3, 5, 4)


def dot(a, b):
    return jnp.dot(a, b, preferred_element_type=F32)


def dot_tn(a, b):
    return lax.dot_general(a, b, (((0,), (0,)), ((), ())), preferred_element_type=F32)


def mask(condition):
    return condition.astype(F32).astype(BF16)


def iota(shape, dim):
    return lax.broadcasted_iota(I32, shape, dim)


def kernel(
    loads_in, stiff_in, linv_in, basis, cinv_in, index_in, left, right,
    out_u, out_r,
    loads, stiff, linv, cinv,
    place_buf, cinv_wide, perm_head, perm_tail, bp, basis_t, basis_full, put_face, pick_coarse,
    face_part, face_got, face_own, sa, ra, head, tail, sc, rc, gd, re, pk, wb, ab, fs, nb, rf, local, first, kept, restricted,
    send_sem, recv_sem, near_recv, far_recv, near_send, far_send, load_sem,
):
    sub = lax.axis_index("sub")
    crow = lax.axis_index("crow")
    ccol = lax.axis_index("ccol")
    core = lax.rem(crow, 2)
    chip = (crow // 2) * 2 + ccol
    g = crow * 2 + ccol
    sy, sz = sub // SIDE, lax.rem(sub, SIDE)
    q1 = sz * (1 - core) + sy * core
    q2 = sy * (1 - core) + sz * core

    def group_peer(k):
        t = lax.rem(g + k, GROUP)
        return t, {"sub": sub, "crow": t // 2, "ccol": lax.rem(t, 2)}

    def plane_at(a, b):
        y = b * (1 - core) + a * core
        z = a * (1 - core) + b * core
        return {"sub": y * SIDE + z, "crow": crow, "ccol": ccol}

    def first_peer(d):
        return plane_at(lax.rem(q1 + d, SIDE), q2)

    def second_peer(d):
        return plane_at(q1, lax.rem(q2 + d, SIDE))

    def far_first(i):
        return 4 + (1 - 2 * lax.rem(i, 2)) * ((i + 1) // 2)

    def plane_peer(k):
        y = lax.rem(sy + far_first(k // SIDE), SIDE)
        z = lax.rem(sz + far_first(lax.rem(k, SIDE)), SIDE)
        return {"sub": y * SIDE + z, "crow": crow, "ccol": ccol}

    def copy(src, dst, s, r, device):
        pltpu.make_async_remote_copy(
            src_ref=src, dst_ref=dst, send_sem=s, recv_sem=r, device_id=device, device_id_type=MESH
        ).start()

    def wait(ref, sem):
        pltpu.make_async_copy(ref, ref, sem).wait()

    def repeat(low, high, step):
        def one(k, carry):
            step(k)
            return carry

        lax.fori_loop(low, high, one, 0)

    def sems(stage, p):
        i = STAGES.index(stage) * 2 + p
        return send_sem.at[i], recv_sem.at[i]

    def to_group(ref_of, dst, stage, p):
        s, r = sems(stage, p)

        def step(k):
            t, device = group_peer(k)
            copy(ref_of(t), dst, s, r, device)

        repeat(1, GROUP, step)

    mine = pl.ds(pl.multiple_of(g * 128, 128), 128)
    seven = pl.ds(0, 7)

    def kinds(p):
        return pl.ds(0, 2) if p == 0 else pl.ds(2, 1)

    arrivals = {
        "basis": lambda p: basis_t.at[:, pl.ds(0, 896)],
        "faces": lambda p: face_got.at[seven],
        "a": lambda p: ra.at[seven],
        "c": lambda p: rc.at[p, seven],
        "e": lambda p: re.at[p, seven],
        "w": lambda p: wb.at[p, :, pl.ds(0, 896)],
        "r": lambda p: rf.at[:, pl.ds(0, 896)],
        "inner": lambda p: nb.at[kinds(p), pl.ds(0, 2), seven],
        "before": lambda p: nb.at[kinds(p), 2],
        "after": lambda p: nb.at[kinds(p), 3],
    }

    def arrived(stage, p):
        wait(arrivals[stage](p), sems(stage, p)[1])

    def spot(half):
        return (q2, q1) if half == 0 else (q1, q2)

    def near_peer(half, d):
        return first_peer(d) if half == 0 else second_peer(d)

    def far_peer(half, d):
        return second_peer(d) if half == 0 else first_peer(d)

    def pipe_start(name, refs):
        i = PIPES.index(name)

        def near(d):
            for half, ref in enumerate(refs):
                block = ref.at[spot(half)]
                copy(block, block, near_send.at[i, half], near_recv.at[i, half, d], near_peer(half, d))

        def far(d):
            for half, ref in enumerate(refs):
                block = ref.at[spot(half)]
                copy(block, block, far_send.at[i, half], far_recv.at[i, half], far_peer(half, d))

        repeat(0, SIDE - 1, lambda k: near(far_first(k)))
        repeat(0, SIDE - 1, lambda k: far(far_first(k)))

    def pipe_forward(name, refs):
        i = PIPES.index(name)
        for e in NEAREST:
            for half, ref in enumerate(refs):
                a, b = spot(half)
                block = ref.at[a, lax.rem(b + SIDE - e, SIDE)]
                wait(block, near_recv.at[i, half, e])

                def far(d):
                    copy(block, block, far_send.at[i, half], far_recv.at[i, half], far_peer(half, d))

                repeat(0, SIDE - 1, lambda k: far(far_first(k)))

    def pipe_wait(name, refs):
        i = PIPES.index(name)
        for half, ref in enumerate(refs):
            wait(ref.at[seven], far_recv.at[i, half])

    def pipe_settle(name, refs):
        i = PIPES.index(name)
        for half, ref in enumerate(refs):
            wait(ref.at[0, seven], near_send.at[i, half])
            wait(ref.at[seven], far_send.at[i, half])

    gd[...] = jnp.zeros(gd.shape, BF16)
    pk[...] = jnp.zeros(pk.shape, BF16)

    barrier = pltpu.get_barrier_semaphore()

    def greet(k):
        for device in (group_peer(k)[1], first_peer(k), second_peer(k)):
            pl.semaphore_signal(barrier, inc=1, device_id=device, device_id_type=MESH)

    repeat(1, SIDE, greet)

    operands = ((stiff_in, stiff), (linv_in, linv), (loads_in, loads), (cinv_in, cinv))
    for i, (outer, inner) in enumerate(operands):
        pltpu.make_async_copy(outer, inner, load_sem.at[i]).start()

    lane_i, down_i = iota((128, 128), 1), iota((128, 128), 0)
    lane, down = lane_i.astype(F32), down_i.astype(F32)
    g_f = g.astype(F32)

    index_lane = jnp.zeros((8, 128), F32)
    for s in range(2):
        shift = mask(iota((MODES, 128), 1) == iota((MODES, 128), 0) + MODES * s)
        index = jnp.broadcast_to(index_in[s : s + 1, :], (8, MODES))
        high = lax.shift_right_logical(index, 6)
        low = index - high * 64
        index_lane += 64.0 * dot(high.astype(F32).astype(BF16), shift)
        index_lane += dot(low.astype(F32).astype(BF16), shift)
    index_lane = jnp.broadcast_to(index_lane[0:1], (128, 128))
    index_lane = jnp.where(lane < OWN, index_lane, -1.0)
    index_down = jnp.transpose(index_lane)

    def block_of(index):
        block = jnp.zeros(index.shape, F32)
        for t in range(1, GROUP):
            block += (index >= t * BLOCK).astype(F32)
        return jnp.where(index < 0, 99.0, block)

    block_lane, block_down = block_of(index_lane), block_of(index_down)
    earlier = (block_lane == block_down) & (down < lane)
    rank = jnp.sum(earlier.astype(F32), axis=0, keepdims=True)
    code_lane = jnp.broadcast_to(block_lane[0:1] * CAP + rank, (128, 128))
    code_down = jnp.transpose(code_lane)
    select_own = mask(code_lane[0:CAP] == down[0:CAP] + g_f * CAP)

    slot = lane - (q1 * HEAD).astype(F32)
    in_head = (code_down == g_f * CAP + slot) & (slot >= 0) & (slot < HEAD)
    slot = lane - (lax.rem(q1, 2) * 64 + q2 * TAIL).astype(F32)
    in_tail = (code_down == g_f * CAP + HEAD + slot) & (slot >= 0) & (slot < TAIL)
    value = index_down - g_f * BLOCK + 1.0
    place_buf[q2, q1, :, 0:128] = jnp.sum(jnp.where(in_head, value, 0.0), axis=0, keepdims=True)
    place_buf[q2, q1, :, 128:256] = jnp.sum(jnp.where(in_tail, value, 0.0), axis=0, keepdims=True)
    place_buf[q2, q1, :, 256:384] = index_lane[0:1]

    basis_own = basis[...].reshape(OWN, 128)
    basis_t[:, mine] = basis_own

    pl.semaphore_wait(barrier, GROUP + 2 * SIDE - 3)

    to_group(lambda t: basis_t.at[:, mine], basis_t.at[:, mine], "basis", 0)
    pipe_start("place", [place_buf])

    for i, (outer, inner) in enumerate(operands):
        pltpu.make_async_copy(outer, inner, load_sem.at[i]).wait()
    for s in range(2):
        for side, rows in enumerate((left, right)):
            row_lane = jnp.broadcast_to(rows[s : s + 1, :].astype(F32), (128, 128))
            put = row_lane == down + 128.0 * g_f
            put_face[s, side] = mask(put)
            pick = mask(jnp.transpose(put.astype(F32)) > 0.5)
            part = dot(pick, stiff[s]).astype(BF16)
            face_part[:, (2 * s + side) * STEP : (2 * s + side + 1) * STEP, :] = part.reshape(
                GROUP, STEP, 1024
            )

    out_row, out_of = iota((128, OWN), 0), iota((128, OWN), 1)
    part_of, within = out_row // STEP, lax.rem(out_row, STEP)
    part_core = lax.rem(part_of // 2, 2)
    part_chip = (part_of // 4) * 2 + lax.rem(part_of, 2)
    wide = (out_of == part_chip * CAP + part_core * STEP + within) & (within < STEP - 8 * part_core)
    cinv_wide[...] = dot(mask(wide), cinv[...]).astype(BF16)
    for s in range(2):
        local[s] = dot(linv[s], loads[s])
        wb[0, s, mine] = local[s].astype(BF16)


    def settle_faces():
        total = face_got[0]
        for t in range(1, GROUP):
            total += face_got[t]
        face_own[...] = total

    arrived("basis", 0)
    for s in range(2):
        restricted[s * MODES : (s + 1) * MODES] = dot(
            basis_t[s * MODES : (s + 1) * MODES, :], loads[s]
        ).astype(BF16)
    rows = dot(select_own[:, 0:OWN], restricted[...]).astype(BF16)

    def spread(p, rows):
        head[(p, *spot(0))] = rows[0:HEAD]
        tail[(p, *spot(1))] = rows[HEAD:CAP]
        pipe_start(PIPES[1 + p], [head.at[p], tail.at[p]])

    spread(0, rows)
    face_got[g] = face_part[g]
    to_group(lambda t: face_part.at[t], face_got.at[g], "faces", 0)
    to_group(lambda t: wb.at[0, :, mine], wb.at[0, :, mine], "w", 0)
    pipe_forward("place", [place_buf])
    pipe_forward("b0", [head.at[0], tail.at[0]])

    pipe_wait("place", [place_buf])
    tall = iota((BLOCK, 128), 0).astype(F32) + 1.0
    for c in range(8):
        where = jnp.sum(place_buf[c, :, 0, 0:128], axis=0, keepdims=True)
        perm_head[:, c * 128 : (c + 1) * 128] = dot(cinv_wide[...], mask(tall == where)).astype(BF16)
    for c in range(4):
        where = jnp.sum(
            place_buf[:, 2 * c, 0, 128:256] + place_buf[:, 2 * c + 1, 0, 128:256], axis=0, keepdims=True
        )
        perm_tail[:, c * 128 : (c + 1) * 128] = dot(cinv_wide[...], mask(tall == where)).astype(BF16)
    for s in range(2):
        for j in range(8):
            shift = mask(iota((MODES, 128), 1) == iota((MODES, 128), 0) + MODES * s)
            turned = dot_tn(basis_t[s * MODES : (s + 1) * MODES, j * 128 : (j + 1) * 128], shift)
            basis_full[s, j * 128 : (j + 1) * 128, :] = turned.astype(BF16)
    select = mask(
        jnp.broadcast_to(code_lane[0:1], (GROUP * CAP, 128)) == iota((GROUP * CAP, 128), 0).astype(F32)
    )
    for s in range(2):
        keep = (iota((OWN, 128), 0) >= s * MODES) & (iota((OWN, 128), 0) < (s + 1) * MODES)
        part = jnp.where(keep, basis_own.astype(F32), 0.0).astype(BF16)
        bp[s] = dot(select[:, 0:OWN], part).astype(BF16)

    def index_of(other):
        y, z = other // SIDE, lax.rem(other, SIDE)
        a = z * (1 - core) + y * core
        b = y * (1 - core) + z * core
        return place_buf[b, a, :, 256:384]

    after_index = index_of(lax.rem(sub + 1, PLANE))
    before_index = index_of(lax.rem(sub + PLANE - 1, PLANE))
    index_near = jnp.where(lane[0:1] < MODES, after_index, before_index)
    index_near = jnp.transpose(jnp.broadcast_to(index_near, (128, 128)))
    for j in range(8):
        column = lane_i + 128 * j
        within = lax.rem(column, STEP)
        row_of = (column // STEP) * OWN + chip * CAP + core * STEP + within
        row_of = jnp.where(within < STEP - 8 * core, row_of, -5)
        for k, index in enumerate((index_down, index_near)):
            chosen = mask(index == row_of.astype(F32))[0:OWN]
            pick_coarse[k * OWN : (k + 1) * OWN, j * 128 : (j + 1) * 128] = chosen

    def coarse_start(p):
        pipe_wait(PIPES[1 + p], [head.at[p], tail.at[p]])
        part = dot(perm_head[...], head[p].reshape(PLANE * HEAD, 128))
        part += dot(perm_tail[...], tail[p].reshape(PLANE * TAIL, 128))
        sc[p] = part.reshape(GROUP, STEP, 128)
        rc[p, g] = sc[p, g]
        to_group(lambda t: sc.at[p, t], rc.at[p, g], "c", p)
        if p == 0:
            arrived("faces", 0)
            settle_faces()
            arrived("w", 0)
            faces_start(0)
        arrived("c", p)
        total = rc[p, 0]
        for t in range(1, GROUP):
            total += rc[p, t]
        gd[p, sub] = total.astype(BF16)
        s, r = sems("d", p)
        for kind, size in enumerate((16, 8)):
            @pl.when(core == kind)
            def _():
                block = gd.at[p, sub, pl.ds(0, size)]
                repeat(0, PLANE - 1, lambda k: copy(block, block, s, r, plane_peer(k)))

    def each_plane(p, which):
        for kind, size in enumerate((16, 8)):
            @pl.when(core == kind)
            def _():
                wait(gd.at[p, pl.ds(0, PLANE - 1), pl.ds(0, size)], sems("d", p)[which])

    def coarse_pick(p):
        each_plane(p, 1)
        found = dot(pick_coarse[...], gd[p].reshape(PLANE * STEP, 128))
        re[p, g] = found.astype(BF16)
        to_group(lambda t: re.at[p, g], re.at[p, g], "e", p)
    def coarse_end(p):
        arrived("e", p)
        picked = re[p, 0].astype(F32)
        for t in range(1, GROUP):
            picked += re[p, t].astype(F32)
        pk[p, 0, 0:OWN] = picked[0:OWN].astype(BF16)
        pk[p, 1, 0:OWN] = picked[OWN : 2 * OWN].astype(BF16)


    def faces_start(p):
        for kind in range(2 * p, 2 + p):
            source = basis_full if kind == 1 else wb.at[p]
            faces = [
                dot(face_own[2 * STEP * s : 2 * STEP * (s + 1)], source[s]).astype(BF16) for s in range(2)
            ]
            nb[kind, 0, g] = faces[1][0:STEP]
            nb[kind, 1, g] = faces[0][STEP : 2 * STEP]
            fs[kind, 0] = faces[0][0:STEP]
            fs[kind, 1] = faces[1][STEP : 2 * STEP]
        s_before, r_before = sems("before", p)
        s_after, r_after = sems("after", p)

        def outward(k):
            t = lax.rem(g + k, GROUP)
            place = {"crow": t // 2, "ccol": lax.rem(t, 2)}
            up = {"sub": lax.rem(sub + 1, PLANE), **place}
            low = {"sub": lax.rem(sub + PLANE - 1, PLANE), **place}
            copy(fs.at[kinds(p), 1], nb.at[kinds(p), 2, g], s_before, r_before, up)
            copy(fs.at[kinds(p), 0], nb.at[kinds(p), 3, g], s_after, r_after, low)

        repeat(0, GROUP, outward)
        inner = nb.at[kinds(p), pl.ds(0, 2), g]
        to_group(lambda t: inner, inner, "inner", p)

    def faces_wait(p):
        for stage in ("inner", "before", "after"):
            arrived(stage, p)

    def face(kind, which):
        return nb[kind, which].reshape(128, 128)

    def residual_local(p):
        kind = 2 * p
        after = (face(kind, 0), face(kind, 3))
        before = (face(kind, 2), face(kind, 1))
        return [
            loads[s, mine].astype(F32)
            - (dot(stiff[s], wb[p, s]) + dot(put_face[s, 0], before[s]) + dot(put_face[s, 1], after[s]))
            for s in range(2)
        ]

    def residual_of(p, early):
        return [early[s] - (dot(ab[s, 0], pk[p, 0]) + dot(ab[s, 1], pk[p, 1])) for s in range(2)]

    coarse_start(0)
    faces_wait(0)
    for s in range(2):
        image = dot(stiff[s], basis_full[s])
        if s == 0:
            ab[s, 0] = (image + dot(put_face[0, 1], face(1, 0))).astype(BF16)
            ab[s, 1] = dot(put_face[0, 0], face(1, 2)).astype(BF16)
        else:
            ab[s, 0] = (image + dot(put_face[1, 0], face(1, 1))).astype(BF16)
            ab[s, 1] = dot(put_face[1, 1], face(1, 3)).astype(BF16)
    early = residual_local(0)
    for s in range(2):
        kept[s] = early[s]
    pieces = [[early[s].astype(BF16) for s in range(2)]] + [[ab[s, k] for s in range(2)] for k in range(2)]
    for k, piece in enumerate(pieces):
        part = dot(bp[0], piece[0]) + dot(bp[1], piece[1])
        sa[:, k] = part.reshape(GROUP, CAP, 128)
    ra[g] = sa[g]
    to_group(lambda t: sa.at[t], ra.at[g], "a", 0)
    coarse_pick(0)
    arrived("a", 0)
    total = ra[0]
    for t in range(1, GROUP):
        total += ra[t]
    coarse_end(0)
    rows = total[0] - dot(total[1].astype(BF16), pk[0, 0]) - dot(total[2].astype(BF16), pk[0, 1])
    spread(1, rows.astype(BF16))
    residual = residual_of(0, [kept[s] for s in range(2)])
    for s in range(2):
        rf[s, mine] = residual[s].astype(BF16)
    to_group(lambda t: rf.at[:, mine], rf.at[:, mine], "r", 0)
    for s in range(2):
        first[s] = local[s] + dot(basis_full[s, mine], pk[0, 0])
    pipe_forward("b1", [head.at[1], tail.at[1]])
    arrived("r", 0)
    for s in range(2):
        first[s] = first[s] + dot(linv[s], rf[s])
        wb[1, s, mine] = first[s].astype(BF16)
    coarse_start(1)
    to_group(lambda t: wb.at[1, :, mine], wb.at[1, :, mine], "w", 1)
    arrived("w", 1)
    faces_start(1)
    coarse_pick(1)
    faces_wait(1)
    early = residual_local(1)
    coarse_end(1)
    for s in range(2):
        out_u[s] = first[s] + dot(basis_full[s, mine], pk[1, 0])
    final = residual_of(1, early)
    for s in range(2):
        out_r[s] = final[s]

    for stage in ("basis", "faces", "a", "r"):
        wait(arrivals[stage](0), sems(stage, 0)[0])
    pipe_settle("place", [place_buf])
    for p in range(2):
        for stage in ("c", "e", "w", "inner", "before", "after"):
            wait(arrivals[stage](p), sems(stage, p)[0])
        each_plane(p, 0)
        pipe_settle(PIPES[1 + p], [head.at[p], tail.at[p]])


def body(loads, stiffness, local_inverse, coarse_basis, coarse_inverse, coarse_index, left, right):
    vmem = pl.BlockSpec(memory_space=pltpu.VMEM)
    away = pl.BlockSpec(memory_space=pl.ANY)
    out = jax.ShapeDtypeStruct((2, 128, 128), F32)
    count = 2 * len(STAGES)
    dma = pltpu.SemaphoreType.DMA
    return pl.pallas_call(
        kernel,
        out_shape=(out, out),
        in_specs=[away, away, away, vmem, away, vmem, vmem, vmem],
        out_specs=(vmem, vmem),
        scratch_shapes=[
            pltpu.VMEM((2, 1024, 128), BF16),
            pltpu.VMEM((2, 128, 1024), BF16),
            pltpu.VMEM((2, 128, 1024), BF16),
            pltpu.VMEM((OWN, BLOCK), BF16),
            pltpu.VMEM((SIDE, SIDE, 1, 384), F32),
            pltpu.VMEM((128, BLOCK), BF16),
            pltpu.VMEM((128, PLANE * HEAD), BF16),
            pltpu.VMEM((128, PLANE * TAIL), BF16),
            pltpu.VMEM((2, GROUP * CAP, 128), BF16),
            pltpu.VMEM((OWN, 1024), BF16),
            pltpu.VMEM((2, 1024, 128), BF16),
            pltpu.VMEM((2, 2, 128, 128), BF16),
            pltpu.VMEM((2 * OWN, PLANE * STEP), BF16),
            pltpu.VMEM((GROUP, 4 * STEP, 1024), BF16),
            pltpu.VMEM((GROUP, 4 * STEP, 1024), BF16),
            pltpu.VMEM((4 * STEP, 1024), BF16),
            pltpu.VMEM((GROUP, 3, CAP, 128), F32),
            pltpu.VMEM((GROUP, 3, CAP, 128), F32),
            pltpu.VMEM((2, SIDE, SIDE, HEAD, 128), BF16),
            pltpu.VMEM((2, SIDE, SIDE, TAIL, 128), BF16),
            pltpu.VMEM((2, GROUP, STEP, 128), F32),
            pltpu.VMEM((2, GROUP, STEP, 128), F32),
            pltpu.VMEM((2, PLANE, STEP, 128), BF16),
            pltpu.VMEM((2, GROUP, 2 * OWN, 128), BF16),
            pltpu.VMEM((2, 2, 128, 128), BF16),
            pltpu.VMEM((2, 2, 1024, 128), BF16),
            pltpu.VMEM((2, 2, 128, 128), BF16),
            pltpu.VMEM((3, 2, STEP, 128), BF16),
            pltpu.VMEM((3, 4, GROUP, STEP, 128), BF16),
            pltpu.VMEM((2, 1024, 128), BF16),
            pltpu.VMEM((2, 128, 128), F32),
            pltpu.VMEM((2, 128, 128), F32),
            pltpu.VMEM((2, 128, 128), F32),
            pltpu.VMEM((OWN, 128), BF16),
            dma((count,)),
            dma((count,)),
            dma((len(PIPES), 2, SIDE)),
            dma((len(PIPES), 2)),
            dma((len(PIPES), 2)),
            dma((len(PIPES), 2)),
            dma((4,)),
        ],
        compiler_params=pltpu.CompilerParams(collective_id=0, has_side_effects=True),
        name="schwarz",
    )(
        loads, stiffness, local_inverse, jnp.swapaxes(coarse_basis, 1, 2), coarse_inverse, coarse_index, left, right
    )


def solution(mesh):
    group = ("crow", "ccol")
    return jax.shard_map(
        body,
        mesh=mesh,
        in_specs=(
            P("sub", None, None),
            P("sub", group, None),
            P("sub", group, None),
            P("sub", group, None),
            P("sub", group),
            P("sub", None),
            P("sub", None),
            P("sub", None),
        ),
        out_specs=(P("sub", group, None), P("sub", group, None)),
        check_vma=False,
    )
```

```python
import jax
import jax.numpy as jnp
from jax import lax
from jax.experimental import pallas as pl
from jax.experimental.pallas import tpu as pltpu
from jax.sharding import PartitionSpec as P

MESH = pl.DeviceIdType.MESH
F32, BF16, I32 = jnp.float32, jnp.bfloat16, jnp.int32
GROUP = 8
PLANE = 64
SIDE = 8
CAP = 24
HEAD, TAIL = 16, 8
BLOCK = 768
OWN = 96
MODES = 48
STEP = 16
STAGES = ("basis", "pair", "faces", "a", "c", "d", "e", "w", "r", "inner", "before", "after")
PIPES = ("place", "b0", "b1")
NEAREST = (1, 7, 2, 6, 3, 5, 4)


def dot(a, b):
    return jnp.dot(a, b, preferred_element_type=F32)


def dot_tn(a, b):
    return lax.dot_general(a, b, (((0,), (0,)), ((), ())), preferred_element_type=F32)


def mask(condition):
    return condition.astype(F32).astype(BF16)


def iota(shape, dim):
    return lax.broadcasted_iota(I32, shape, dim)


def kernel(
    loads_in, stiff_in, linv_in, basis, cinv_in, index_in, left, right,
    out_u, out_r,
    loads, stiff, linv, cinv,
    place_buf, cinv_wide, perm_head, perm_tail, bp, basis_t, basis_full, put_face, pick_coarse,
    face_part, face_pair, face_got, face_own, sa, ra, head, tail, sc, rc, gd, re, pk, wb, ab, fs, nb, rf, local, first, kept, restricted,
    send_sem, recv_sem, near_recv, far_recv, near_send, far_send, load_sem,
):
    sub = lax.axis_index("sub")
    crow = lax.axis_index("crow")
    ccol = lax.axis_index("ccol")
    core = lax.rem(crow, 2)
    chip = (crow // 2) * 2 + ccol
    g = crow * 2 + ccol
    sy, sz = sub // SIDE, lax.rem(sub, SIDE)
    q1 = sz * (1 - core) + sy * core
    q2 = sy * (1 - core) + sz * core

    def group_peer(k):
        t = lax.rem(g + k, GROUP)
        return t, {"sub": sub, "crow": t // 2, "ccol": lax.rem(t, 2)}

    def plane_at(a, b):
        y = b * (1 - core) + a * core
        z = a * (1 - core) + b * core
        return {"sub": y * SIDE + z, "crow": crow, "ccol": ccol}

    def first_peer(d):
        return plane_at(lax.rem(q1 + d, SIDE), q2)

    def second_peer(d):
        return plane_at(q1, lax.rem(q2 + d, SIDE))

    def far_first(i):
        return 4 + (1 - 2 * lax.rem(i, 2)) * ((i + 1) // 2)

    def plane_peer(k):
        y = lax.rem(sy + far_first(k // SIDE), SIDE)
        z = lax.rem(sz + far_first(lax.rem(k, SIDE)), SIDE)
        return {"sub": y * SIDE + z, "crow": crow, "ccol": ccol}

    def copy(src, dst, s, r, device):
        pltpu.make_async_remote_copy(
            src_ref=src, dst_ref=dst, send_sem=s, recv_sem=r, device_id=device, device_id_type=MESH
        ).start()

    def wait(ref, sem):
        pltpu.make_async_copy(ref, ref, sem).wait()

    def repeat(low, high, step):
        def one(k, carry):
            step(k)
            return carry

        lax.fori_loop(low, high, one, 0)

    def sems(stage, p):
        i = STAGES.index(stage) * 2 + p
        return send_sem.at[i], recv_sem.at[i]

    def to_group(ref_of, dst, stage, p):
        s, r = sems(stage, p)

        def step(k):
            t, device = group_peer(k)
            copy(ref_of(t), dst, s, r, device)

        repeat(1, GROUP, step)

    mine = pl.ds(pl.multiple_of(g * 128, 128), 128)
    seven = pl.ds(0, 7)

    def kinds(p):
        return pl.ds(0, 2) if p == 0 else pl.ds(2, 1)

    arrivals = {
        "basis": lambda p: basis_t.at[:, pl.ds(0, 896)],
        "pair": lambda p: face_pair,
        "faces": lambda p: face_got.at[pl.ds(0, 3)],
        "a": lambda p: ra.at[seven],
        "c": lambda p: rc.at[p, seven],
        "e": lambda p: re.at[p, seven],
        "w": lambda p: wb.at[p, :, pl.ds(0, 896)],
        "r": lambda p: rf.at[:, pl.ds(0, 896)],
        "inner": lambda p: nb.at[kinds(p), pl.ds(0, 2), seven],
        "before": lambda p: nb.at[kinds(p), 2],
        "after": lambda p: nb.at[kinds(p), 3],
    }

    def arrived(stage, p):
        wait(arrivals[stage](p), sems(stage, p)[1])

    def spot(half):
        return (q2, q1) if half == 0 else (q1, q2)

    def near_peer(half, d):
        return first_peer(d) if half == 0 else second_peer(d)

    def far_peer(half, d):
        return second_peer(d) if half == 0 else first_peer(d)

    def pipe_start(name, refs):
        i = PIPES.index(name)

        def near(d):
            for half, ref in enumerate(refs):
                block = ref.at[spot(half)]
                copy(block, block, near_send.at[i, half], near_recv.at[i, half, d], near_peer(half, d))

        def far(d):
            for half, ref in enumerate(refs):
                block = ref.at[spot(half)]
                copy(block, block, far_send.at[i, half], far_recv.at[i, half], far_peer(half, d))

        repeat(0, SIDE - 1, lambda k: near(far_first(k)))
        repeat(0, SIDE - 1, lambda k: far(far_first(k)))

    def pipe_forward(name, refs):
        i = PIPES.index(name)
        for e in NEAREST:
            for half, ref in enumerate(refs):
                a, b = spot(half)
                block = ref.at[a, lax.rem(b + SIDE - e, SIDE)]
                wait(block, near_recv.at[i, half, e])

                def far(d):
                    copy(block, block, far_send.at[i, half], far_recv.at[i, half], far_peer(half, d))

                repeat(0, SIDE - 1, lambda k: far(far_first(k)))

    def pipe_wait(name, refs):
        i = PIPES.index(name)
        for half, ref in enumerate(refs):
            wait(ref.at[seven], far_recv.at[i, half])

    def pipe_settle(name, refs):
        i = PIPES.index(name)
        for half, ref in enumerate(refs):
            wait(ref.at[0, seven], near_send.at[i, half])
            wait(ref.at[seven], far_send.at[i, half])

    gd[...] = jnp.zeros(gd.shape, BF16)
    pk[...] = jnp.zeros(pk.shape, BF16)

    barrier = pltpu.get_barrier_semaphore()

    def greet(k):
        for device in (group_peer(k)[1], first_peer(k), second_peer(k)):
            pl.semaphore_signal(barrier, inc=1, device_id=device, device_id_type=MESH)

    repeat(1, SIDE, greet)

    operands = ((stiff_in, stiff), (linv_in, linv), (loads_in, loads), (cinv_in, cinv))
    for i, (outer, inner) in enumerate(operands):
        pltpu.make_async_copy(outer, inner, load_sem.at[i]).start()

    lane_i, down_i = iota((128, 128), 1), iota((128, 128), 0)
    lane, down = lane_i.astype(F32), down_i.astype(F32)
    g_f = g.astype(F32)

    index_lane = jnp.zeros((8, 128), F32)
    for s in range(2):
        shift = mask(iota((MODES, 128), 1) == iota((MODES, 128), 0) + MODES * s)
        index = jnp.broadcast_to(index_in[s : s + 1, :], (8, MODES))
        high = lax.shift_right_logical(index, 6)
        low = index - high * 64
        index_lane += 64.0 * dot(high.astype(F32).astype(BF16), shift)
        index_lane += dot(low.astype(F32).astype(BF16), shift)
    index_lane = jnp.broadcast_to(index_lane[0:1], (128, 128))
    index_lane = jnp.where(lane < OWN, index_lane, -1.0)
    index_down = jnp.transpose(index_lane)

    def block_of(index):
        block = jnp.zeros(index.shape, F32)
        for t in range(1, GROUP):
            block += (index >= t * BLOCK).astype(F32)
        return jnp.where(index < 0, 99.0, block)

    block_lane, block_down = block_of(index_lane), block_of(index_down)
    earlier = (block_lane == block_down) & (down < lane)
    rank = jnp.sum(earlier.astype(F32), axis=0, keepdims=True)
    code_lane = jnp.broadcast_to(block_lane[0:1] * CAP + rank, (128, 128))
    code_down = jnp.transpose(code_lane)
    select_own = mask(code_lane[0:CAP] == down[0:CAP] + g_f * CAP)

    slot = lane - (q1 * HEAD).astype(F32)
    in_head = (code_down == g_f * CAP + slot) & (slot >= 0) & (slot < HEAD)
    slot = lane - (lax.rem(q1, 2) * 64 + q2 * TAIL).astype(F32)
    in_tail = (code_down == g_f * CAP + HEAD + slot) & (slot >= 0) & (slot < TAIL)
    value = index_down - g_f * BLOCK + 1.0
    place_buf[q2, q1, :, 0:128] = jnp.sum(jnp.where(in_head, value, 0.0), axis=0, keepdims=True)
    place_buf[q2, q1, :, 128:256] = jnp.sum(jnp.where(in_tail, value, 0.0), axis=0, keepdims=True)
    place_buf[q2, q1, :, 256:384] = index_lane[0:1]

    basis_own = basis[...].reshape(OWN, 128)
    basis_t[:, mine] = basis_own

    pl.semaphore_wait(barrier, GROUP + 2 * SIDE - 3)

    to_group(lambda t: basis_t.at[:, mine], basis_t.at[:, mine], "basis", 0)
    pipe_start("place", [place_buf])

    for i, (outer, inner) in enumerate(operands):
        pltpu.make_async_copy(outer, inner, load_sem.at[i]).wait()
    for s in range(2):
        for side, rows in enumerate((left, right)):
            row_lane = jnp.broadcast_to(rows[s : s + 1, :].astype(F32), (128, 128))
            put = row_lane == down + 128.0 * g_f
            put_face[s, side] = mask(put)
            pick = mask(jnp.transpose(put.astype(F32)) > 0.5)
            part = dot(pick, stiff[s]).astype(BF16)
            face_part[:, (2 * s + side) * STEP : (2 * s + side + 1) * STEP, :] = part.reshape(
                GROUP, STEP, 1024
            )

    partner = {"sub": sub, "crow": crow + 1 - 2 * core, "ccol": ccol}
    for half in range(2):
        theirs = face_part.at[pl.ds(4 * half + 2 * (1 - core), 2)]
        copy(theirs, face_pair.at[pl.ds(2 * half, 2)], *sems("pair", 0), partner)
    for s in range(2):
        local[s] = dot(linv[s], loads[s])
        wb[0, s, mine] = local[s].astype(BF16)
    to_group(lambda t: wb.at[0, :, mine], wb.at[0, :, mine], "w", 0)
    out_row, out_of = iota((128, OWN), 0), iota((128, OWN), 1)
    part_of, within = out_row // STEP, lax.rem(out_row, STEP)
    part_core = lax.rem(part_of // 2, 2)
    part_chip = (part_of // 4) * 2 + lax.rem(part_of, 2)
    wide = (out_of == part_chip * CAP + part_core * STEP + within) & (within < STEP - 8 * part_core)
    cinv_wide[...] = dot(mask(wide), cinv[...]).astype(BF16)


    def settle_faces():
        face_own[...] = face_got[0] + face_got[1] + face_got[2] + face_got[3]

    def pass_faces():
        arrived("pair", 0)
        for half in range(2):
            ours = pl.ds(4 * half + 2 * core, 2)
            face_part[ours] = face_part[ours] + face_pair[2 * half : 2 * half + 2]
        face_got[chip] = face_part[g]

        def step(k):
            other = lax.rem(chip + k, 4)
            row, column = (other // 2) * 2 + core, lax.rem(other, 2)
            device = {"sub": sub, "crow": row, "ccol": column}
            copy(face_part.at[row * 2 + column], face_got.at[chip], *sems("faces", 0), device)

        repeat(1, 4, step)

    pass_faces()
    arrived("basis", 0)
    for s in range(2):
        restricted[s * MODES : (s + 1) * MODES] = dot(
            basis_t[s * MODES : (s + 1) * MODES, :], loads[s]
        ).astype(BF16)
    rows = dot(select_own[:, 0:OWN], restricted[...]).astype(BF16)

    def spread(p, rows):
        head[(p, *spot(0))] = rows[0:HEAD]
        tail[(p, *spot(1))] = rows[HEAD:CAP]
        pipe_start(PIPES[1 + p], [head.at[p], tail.at[p]])

    spread(0, rows)
    pipe_forward("place", [place_buf])
    pipe_forward("b0", [head.at[0], tail.at[0]])

    pipe_wait("place", [place_buf])
    tall = iota((BLOCK, 128), 0).astype(F32) + 1.0
    for c in range(8):
        where = jnp.sum(place_buf[c, :, 0, 0:128], axis=0, keepdims=True)
        perm_head[:, c * 128 : (c + 1) * 128] = dot(cinv_wide[...], mask(tall == where)).astype(BF16)
    for c in range(4):
        where = jnp.sum(
            place_buf[:, 2 * c, 0, 128:256] + place_buf[:, 2 * c + 1, 0, 128:256], axis=0, keepdims=True
        )
        perm_tail[:, c * 128 : (c + 1) * 128] = dot(cinv_wide[...], mask(tall == where)).astype(BF16)
    for s in range(2):
        for j in range(8):
            shift = mask(iota((MODES, 128), 1) == iota((MODES, 128), 0) + MODES * s)
            turned = dot_tn(basis_t[s * MODES : (s + 1) * MODES, j * 128 : (j + 1) * 128], shift)
            basis_full[s, j * 128 : (j + 1) * 128, :] = turned.astype(BF16)
    select = mask(
        jnp.broadcast_to(code_lane[0:1], (GROUP * CAP, 128)) == iota((GROUP * CAP, 128), 0).astype(F32)
    )
    for s in range(2):
        keep = (iota((OWN, 128), 0) >= s * MODES) & (iota((OWN, 128), 0) < (s + 1) * MODES)
        part = jnp.where(keep, basis_own.astype(F32), 0.0).astype(BF16)
        bp[s] = dot(select[:, 0:OWN], part).astype(BF16)

    def index_of(other):
        y, z = other // SIDE, lax.rem(other, SIDE)
        a = z * (1 - core) + y * core
        b = y * (1 - core) + z * core
        return place_buf[b, a, :, 256:384]

    after_index = index_of(lax.rem(sub + 1, PLANE))
    before_index = index_of(lax.rem(sub + PLANE - 1, PLANE))
    index_near = jnp.where(lane[0:1] < MODES, after_index, before_index)
    index_near = jnp.transpose(jnp.broadcast_to(index_near, (128, 128)))
    for j in range(8):
        column = lane_i + 128 * j
        within = lax.rem(column, STEP)
        row_of = (column // STEP) * OWN + chip * CAP + core * STEP + within
        row_of = jnp.where(within < STEP - 8 * core, row_of, -5)
        for k, index in enumerate((index_down, index_near)):
            chosen = mask(index == row_of.astype(F32))[0:OWN]
            pick_coarse[k * OWN : (k + 1) * OWN, j * 128 : (j + 1) * 128] = chosen

    def coarse_start(p):
        pipe_wait(PIPES[1 + p], [head.at[p], tail.at[p]])
        part = dot(perm_head[...], head[p].reshape(PLANE * HEAD, 128))
        part += dot(perm_tail[...], tail[p].reshape(PLANE * TAIL, 128))
        sc[p] = part.reshape(GROUP, STEP, 128)
        rc[p, g] = sc[p, g]
        to_group(lambda t: sc.at[p, t], rc.at[p, g], "c", p)
        if p == 0:
            arrived("faces", 0)
            settle_faces()
            arrived("w", 0)
            faces_start(0)
        arrived("c", p)
        total = rc[p, 0]
        for t in range(1, GROUP):
            total += rc[p, t]
        gd[p, sub] = total.astype(BF16)
        s, r = sems("d", p)
        for kind, size in enumerate((16, 8)):
            @pl.when(core == kind)
            def _():
                block = gd.at[p, sub, pl.ds(0, size)]
                repeat(0, PLANE - 1, lambda k: copy(block, block, s, r, plane_peer(k)))

    def each_plane(p, which):
        for kind, size in enumerate((16, 8)):
            @pl.when(core == kind)
            def _():
                wait(gd.at[p, pl.ds(0, PLANE - 1), pl.ds(0, size)], sems("d", p)[which])

    def coarse_pick(p):
        each_plane(p, 1)
        found = dot(pick_coarse[...], gd[p].reshape(PLANE * STEP, 128))
        re[p, g] = found.astype(BF16)
        to_group(lambda t: re.at[p, g], re.at[p, g], "e", p)
    def coarse_end(p):
        arrived("e", p)
        picked = re[p, 0].astype(F32)
        for t in range(1, GROUP):
            picked += re[p, t].astype(F32)
        pk[p, 0, 0:OWN] = picked[0:OWN].astype(BF16)
        pk[p, 1, 0:OWN] = picked[OWN : 2 * OWN].astype(BF16)


    def faces_start(p):
        for kind in range(2 * p, 2 + p):
            source = basis_full if kind == 1 else wb.at[p]
            faces = [
                dot(face_own[2 * STEP * s : 2 * STEP * (s + 1)], source[s]).astype(BF16) for s in range(2)
            ]
            nb[kind, 0, g] = faces[1][0:STEP]
            nb[kind, 1, g] = faces[0][STEP : 2 * STEP]
            fs[kind, 0] = faces[0][0:STEP]
            fs[kind, 1] = faces[1][STEP : 2 * STEP]
        s_before, r_before = sems("before", p)
        s_after, r_after = sems("after", p)

        def outward(k):
            t = lax.rem(g + k, GROUP)
            place = {"crow": t // 2, "ccol": lax.rem(t, 2)}
            up = {"sub": lax.rem(sub + 1, PLANE), **place}
            low = {"sub": lax.rem(sub + PLANE - 1, PLANE), **place}
            copy(fs.at[kinds(p), 1], nb.at[kinds(p), 2, g], s_before, r_before, up)
            copy(fs.at[kinds(p), 0], nb.at[kinds(p), 3, g], s_after, r_after, low)

        repeat(0, GROUP, outward)
        inner = nb.at[kinds(p), pl.ds(0, 2), g]
        to_group(lambda t: inner, inner, "inner", p)

    def faces_wait(p):
        for stage in ("inner", "before", "after"):
            arrived(stage, p)

    def face(kind, which):
        return nb[kind, which].reshape(128, 128)

    def residual_local(p):
        kind = 2 * p
        after = (face(kind, 0), face(kind, 3))
        before = (face(kind, 2), face(kind, 1))
        return [
            loads[s, mine].astype(F32)
            - (dot(stiff[s], wb[p, s]) + dot(put_face[s, 0], before[s]) + dot(put_face[s, 1], after[s]))
            for s in range(2)
        ]

    def residual_of(p, early):
        return [early[s] - (dot(ab[s, 0], pk[p, 0]) + dot(ab[s, 1], pk[p, 1])) for s in range(2)]

    coarse_start(0)
    faces_wait(0)
    for s in range(2):
        image = dot(stiff[s], basis_full[s])
        if s == 0:
            ab[s, 0] = (image + dot(put_face[0, 1], face(1, 0))).astype(BF16)
            ab[s, 1] = dot(put_face[0, 0], face(1, 2)).astype(BF16)
        else:
            ab[s, 0] = (image + dot(put_face[1, 0], face(1, 1))).astype(BF16)
            ab[s, 1] = dot(put_face[1, 1], face(1, 3)).astype(BF16)
    early = residual_local(0)
    for s in range(2):
        kept[s] = early[s]
    pieces = [[early[s].astype(BF16) for s in range(2)]] + [[ab[s, k] for s in range(2)] for k in range(2)]
    for k, piece in enumerate(pieces):
        part = dot(bp[0], piece[0]) + dot(bp[1], piece[1])
        sa[:, k] = part.reshape(GROUP, CAP, 128)
    ra[g] = sa[g]
    to_group(lambda t: sa.at[t], ra.at[g], "a", 0)
    coarse_pick(0)
    arrived("a", 0)
    total = ra[0]
    for t in range(1, GROUP):
        total += ra[t]
    coarse_end(0)
    rows = total[0] - dot(total[1].astype(BF16), pk[0, 0]) - dot(total[2].astype(BF16), pk[0, 1])
    spread(1, rows.astype(BF16))
    residual = residual_of(0, [kept[s] for s in range(2)])
    for s in range(2):
        rf[s, mine] = residual[s].astype(BF16)
    to_group(lambda t: rf.at[:, mine], rf.at[:, mine], "r", 0)
    for s in range(2):
        first[s] = local[s] + dot(basis_full[s, mine], pk[0, 0])
    pipe_forward("b1", [head.at[1], tail.at[1]])
    arrived("r", 0)
    for s in range(2):
        first[s] = first[s] + dot(linv[s], rf[s])
        wb[1, s, mine] = first[s].astype(BF16)
    coarse_start(1)
    to_group(lambda t: wb.at[1, :, mine], wb.at[1, :, mine], "w", 1)
    arrived("w", 1)
    faces_start(1)
    coarse_pick(1)
    faces_wait(1)
    early = residual_local(1)
    coarse_end(1)
    for s in range(2):
        out_u[s] = first[s] + dot(basis_full[s, mine], pk[1, 0])
    final = residual_of(1, early)
    for s in range(2):
        out_r[s] = final[s]

    for stage in ("basis", "pair", "faces", "a", "r"):
        wait(arrivals[stage](0), sems(stage, 0)[0])
    pipe_settle("place", [place_buf])
    for p in range(2):
        for stage in ("c", "e", "w", "inner", "before", "after"):
            wait(arrivals[stage](p), sems(stage, p)[0])
        each_plane(p, 0)
        pipe_settle(PIPES[1 + p], [head.at[p], tail.at[p]])


def body(loads, stiffness, local_inverse, coarse_basis, coarse_inverse, coarse_index, left, right):
    vmem = pl.BlockSpec(memory_space=pltpu.VMEM)
    away = pl.BlockSpec(memory_space=pl.ANY)
    out = jax.ShapeDtypeStruct((2, 128, 128), F32)
    count = 2 * len(STAGES)
    dma = pltpu.SemaphoreType.DMA
    return pl.pallas_call(
        kernel,
        out_shape=(out, out),
        in_specs=[away, away, away, vmem, away, vmem, vmem, vmem],
        out_specs=(vmem, vmem),
        scratch_shapes=[
            pltpu.VMEM((2, 1024, 128), BF16),
            pltpu.VMEM((2, 128, 1024), BF16),
            pltpu.VMEM((2, 128, 1024), BF16),
            pltpu.VMEM((OWN, BLOCK), BF16),
            pltpu.VMEM((SIDE, SIDE, 1, 384), F32),
            pltpu.VMEM((128, BLOCK), BF16),
            pltpu.VMEM((128, PLANE * HEAD), BF16),
            pltpu.VMEM((128, PLANE * TAIL), BF16),
            pltpu.VMEM((2, GROUP * CAP, 128), BF16),
            pltpu.VMEM((OWN, 1024), BF16),
            pltpu.VMEM((2, 1024, 128), BF16),
            pltpu.VMEM((2, 2, 128, 128), BF16),
            pltpu.VMEM((2 * OWN, PLANE * STEP), BF16),
            pltpu.VMEM((GROUP, 4 * STEP, 1024), BF16),
            pltpu.VMEM((4, 4 * STEP, 1024), BF16),
            pltpu.VMEM((4, 4 * STEP, 1024), BF16),
            pltpu.VMEM((4 * STEP, 1024), BF16),
            pltpu.VMEM((GROUP, 3, CAP, 128), F32),
            pltpu.VMEM((GROUP, 3, CAP, 128), F32),
            pltpu.VMEM((2, SIDE, SIDE, HEAD, 128), BF16),
            pltpu.VMEM((2, SIDE, SIDE, TAIL, 128), BF16),
            pltpu.VMEM((2, GROUP, STEP, 128), F32),
            pltpu.VMEM((2, GROUP, STEP, 128), F32),
            pltpu.VMEM((2, PLANE, STEP, 128), BF16),
            pltpu.VMEM((2, GROUP, 2 * OWN, 128), BF16),
            pltpu.VMEM((2, 2, 128, 128), BF16),
            pltpu.VMEM((2, 2, 1024, 128), BF16),
            pltpu.VMEM((2, 2, 128, 128), BF16),
            pltpu.VMEM((3, 2, STEP, 128), BF16),
            pltpu.VMEM((3, 4, GROUP, STEP, 128), BF16),
            pltpu.VMEM((2, 1024, 128), BF16),
            pltpu.VMEM((2, 128, 128), F32),
            pltpu.VMEM((2, 128, 128), F32),
            pltpu.VMEM((2, 128, 128), F32),
            pltpu.VMEM((OWN, 128), BF16),
            dma((count,)),
            dma((count,)),
            dma((len(PIPES), 2, SIDE)),
            dma((len(PIPES), 2)),
            dma((len(PIPES), 2)),
            dma((len(PIPES), 2)),
            dma((4,)),
        ],
        compiler_params=pltpu.CompilerParams(collective_id=0, has_side_effects=True),
        name="schwarz",
    )(
        loads, stiffness, local_inverse, jnp.swapaxes(coarse_basis, 1, 2), coarse_inverse, coarse_index, left, right
    )


def solution(mesh):
    group = ("crow", "ccol")
    return jax.shard_map(
        body,
        mesh=mesh,
        in_specs=(
            P("sub", None, None),
            P("sub", group, None),
            P("sub", group, None),
            P("sub", group, None),
            P("sub", group),
            P("sub", None),
            P("sub", None),
            P("sub", None),
        ),
        out_specs=(P("sub", group, None), P("sub", group, None)),
        check_vma=False,
    )
```

```python
import jax
import jax.numpy as jnp
from jax import lax
from jax.experimental import pallas as pl
from jax.experimental.pallas import tpu as pltpu
from jax.sharding import PartitionSpec as P

MESH = pl.DeviceIdType.MESH
F32, BF16, I32 = jnp.float32, jnp.bfloat16, jnp.int32
GROUP = 8
PLANE = 64
SIDE = 8
CAP = 24
HEAD, TAIL = 16, 8
BLOCK = 768
OWN = 96
MODES = 48
STEP = 16
STAGES = ("basis", "pair", "faces", "a", "c", "d", "e", "w", "r", "inner", "before", "after")
PIPES = ("place", "b0", "b1")
NEAREST = (1, 7, 2, 6, 3, 5, 4)


def dot(a, b):
    return jnp.dot(a, b, preferred_element_type=F32)


def dot_tn(a, b):
    return lax.dot_general(a, b, (((0,), (0,)), ((), ())), preferred_element_type=F32)


def mask(condition):
    return condition.astype(F32).astype(BF16)


def iota(shape, dim):
    return lax.broadcasted_iota(I32, shape, dim)


def kernel(
    loads_in, stiff_in, linv_in, basis_in, cinv_in, index_in, left_in, right_in,
    out,
    loads, stiff, linv, cinv, index_own, basis, left, right,
    place_buf, cinv_wide, perm_head, perm_tail, bp, basis_t, basis_full, put_face, pick_coarse,
    face_part, face_pair, face_got, face_own, sa, ra, head, tail, sc, rc, gd, re, pk, wb, ab, fs, nb, rf, local, first, kept, restricted,
    send_sem, recv_sem, near_recv, far_recv, near_send, far_send, load_sem,
):
    sub = lax.axis_index("sub")
    crow = lax.axis_index("crow")
    ccol = lax.axis_index("ccol")
    core = lax.rem(crow, 2)
    chip = (crow // 2) * 2 + ccol
    g = crow * 2 + ccol
    sy, sz = sub // SIDE, lax.rem(sub, SIDE)
    q1 = sz * (1 - core) + sy * core
    q2 = sy * (1 - core) + sz * core

    def group_peer(k):
        t = lax.rem(g + k, GROUP)
        return t, {"sub": sub, "crow": t // 2, "ccol": lax.rem(t, 2)}

    def plane_at(a, b):
        y = b * (1 - core) + a * core
        z = a * (1 - core) + b * core
        return {"sub": y * SIDE + z, "crow": crow, "ccol": ccol}

    def first_peer(d):
        return plane_at(lax.rem(q1 + d, SIDE), q2)

    def second_peer(d):
        return plane_at(q1, lax.rem(q2 + d, SIDE))

    def far_first(i):
        return 4 + (1 - 2 * lax.rem(i, 2)) * ((i + 1) // 2)

    def plane_peer(k):
        y = lax.rem(sy + far_first(k // SIDE), SIDE)
        z = lax.rem(sz + far_first(lax.rem(k, SIDE)), SIDE)
        return {"sub": y * SIDE + z, "crow": crow, "ccol": ccol}

    def copy(src, dst, s, r, device):
        pltpu.make_async_remote_copy(
            src_ref=src, dst_ref=dst, send_sem=s, recv_sem=r, device_id=device, device_id_type=MESH
        ).start()

    def wait(ref, sem):
        pltpu.make_async_copy(ref, ref, sem).wait()

    def repeat(low, high, step):
        def one(k, carry):
            step(k)
            return carry

        lax.fori_loop(low, high, one, 0)

    def sems(stage, p):
        i = STAGES.index(stage) * 2 + p
        return send_sem.at[i], recv_sem.at[i]

    def to_group(ref_of, dst, stage, p):
        s, r = sems(stage, p)

        def step(k):
            t, device = group_peer(k)
            copy(ref_of(t), dst, s, r, device)

        repeat(1, GROUP, step)

    mine = pl.ds(pl.multiple_of(g * 128, 128), 128)
    seven = pl.ds(0, 7)

    def kinds(p):
        return pl.ds(0, 2) if p == 0 else pl.ds(2, 1)

    arrivals = {
        "basis": lambda p: basis_t.at[:, pl.ds(0, 896)],
        "pair": lambda p: face_pair,
        "faces": lambda p: face_got.at[pl.ds(0, 3)],
        "a": lambda p: ra.at[seven],
        "c": lambda p: rc.at[p, seven],
        "e": lambda p: re.at[p, seven],
        "w": lambda p: wb.at[p, :, pl.ds(0, 896)],
        "r": lambda p: rf.at[:, pl.ds(0, 896)],
        "inner": lambda p: nb.at[kinds(p), pl.ds(0, 2), seven],
        "before": lambda p: nb.at[kinds(p), 2],
        "after": lambda p: nb.at[kinds(p), 3],
    }

    def arrived(stage, p):
        wait(arrivals[stage](p), sems(stage, p)[1])

    def spot(half):
        return (q2, q1) if half == 0 else (q1, q2)

    def near_peer(half, d):
        return first_peer(d) if half == 0 else second_peer(d)

    def far_peer(half, d):
        return second_peer(d) if half == 0 else first_peer(d)

    def pipe_start(name, refs):
        i = PIPES.index(name)

        def near(d):
            for half, ref in enumerate(refs):
                block = ref.at[spot(half)]
                copy(block, block, near_send.at[i, half], near_recv.at[i, half, d], near_peer(half, d))

        def far(d):
            for half, ref in enumerate(refs):
                block = ref.at[spot(half)]
                copy(block, block, far_send.at[i, half], far_recv.at[i, half], far_peer(half, d))

        repeat(0, SIDE - 1, lambda k: near(far_first(k)))
        repeat(0, SIDE - 1, lambda k: far(far_first(k)))

    def pipe_forward(name, refs):
        i = PIPES.index(name)
        for e in NEAREST:
            for half, ref in enumerate(refs):
                a, b = spot(half)
                block = ref.at[a, lax.rem(b + SIDE - e, SIDE)]
                wait(block, near_recv.at[i, half, e])

                def far(d):
                    copy(block, block, far_send.at[i, half], far_recv.at[i, half], far_peer(half, d))

                repeat(0, SIDE - 1, lambda k: far(far_first(k)))

    def pipe_wait(name, refs):
        i = PIPES.index(name)
        for half, ref in enumerate(refs):
            wait(ref.at[seven], far_recv.at[i, half])

    def pipe_settle(name, refs):
        i = PIPES.index(name)
        for half, ref in enumerate(refs):
            wait(ref.at[0, seven], near_send.at[i, half])
            wait(ref.at[seven], far_send.at[i, half])

    barrier = pltpu.get_barrier_semaphore()

    def greet(k):
        for device in (group_peer(k)[1], first_peer(k), second_peer(k)):
            pl.semaphore_signal(barrier, inc=1, device_id=device, device_id_type=MESH)

    repeat(1, SIDE, greet)

    operands = ((stiff_in, stiff), (linv_in, linv), (loads_in, loads), (cinv_in, cinv), (left_in, left), (right_in, right))
    urgent = ((index_in, index_own), (basis_in, basis))
    for i, (outer, inner) in enumerate(urgent):
        pltpu.make_async_copy(outer, inner, load_sem.at[len(operands) + i]).start()
    for i, (outer, inner) in enumerate(operands):
        pltpu.make_async_copy(outer, inner, load_sem.at[i]).start()

    gd[...] = jnp.zeros(gd.shape, BF16)
    pk[...] = jnp.zeros(pk.shape, BF16)
    for i, (outer, inner) in enumerate(urgent):
        pltpu.make_async_copy(outer, inner, load_sem.at[len(operands) + i]).wait()

    lane_i, down_i = iota((128, 128), 1), iota((128, 128), 0)
    lane, down = lane_i.astype(F32), down_i.astype(F32)
    g_f = g.astype(F32)

    index_lane = jnp.zeros((8, 128), F32)
    for s in range(2):
        shift = mask(iota((MODES, 128), 1) == iota((MODES, 128), 0) + MODES * s)
        index = jnp.broadcast_to(index_own[s : s + 1, :], (8, MODES))
        high = lax.shift_right_logical(index, 6)
        low = index - high * 64
        index_lane += 64.0 * dot(high.astype(F32).astype(BF16), shift)
        index_lane += dot(low.astype(F32).astype(BF16), shift)
    index_lane = jnp.broadcast_to(index_lane[0:1], (128, 128))
    index_lane = jnp.where(lane < OWN, index_lane, -1.0)
    index_down = jnp.transpose(index_lane)

    def block_of(index):
        block = jnp.zeros(index.shape, F32)
        for t in range(1, GROUP):
            block += (index >= t * BLOCK).astype(F32)
        return jnp.where(index < 0, 99.0, block)

    block_lane, block_down = block_of(index_lane), block_of(index_down)
    earlier = (block_lane == block_down) & (down < lane)
    rank = jnp.sum(earlier.astype(F32), axis=0, keepdims=True)
    code_lane = jnp.broadcast_to(block_lane[0:1] * CAP + rank, (128, 128))
    code_down = jnp.transpose(code_lane)
    select_own = mask(code_lane[0:CAP] == down[0:CAP] + g_f * CAP)

    slot = lane - (q1 * HEAD).astype(F32)
    in_head = (code_down == g_f * CAP + slot) & (slot >= 0) & (slot < HEAD)
    slot = lane - (lax.rem(q1, 2) * 64 + q2 * TAIL).astype(F32)
    in_tail = (code_down == g_f * CAP + HEAD + slot) & (slot >= 0) & (slot < TAIL)
    value = index_down - g_f * BLOCK + 1.0
    place_buf[q2, q1, :, 0:128] = jnp.sum(jnp.where(in_head, value, 0.0), axis=0, keepdims=True)
    place_buf[q2, q1, :, 128:256] = jnp.sum(jnp.where(in_tail, value, 0.0), axis=0, keepdims=True)
    place_buf[q2, q1, :, 256:384] = index_lane[0:1]

    basis_own = basis[...].reshape(OWN, 128)
    basis_t[:, mine] = basis_own

    pl.semaphore_wait(barrier, GROUP + 2 * SIDE - 3)

    to_group(lambda t: basis_t.at[:, mine], basis_t.at[:, mine], "basis", 0)
    pipe_start("place", [place_buf])

    for i, (outer, inner) in enumerate(operands):
        pltpu.make_async_copy(outer, inner, load_sem.at[i]).wait()
    for s in range(2):
        for side, rows in enumerate((left, right)):
            row_lane = jnp.broadcast_to(rows[s : s + 1, :].astype(F32), (128, 128))
            put = row_lane == down + 128.0 * g_f
            put_face[s, side] = mask(put)
            pick = mask(jnp.transpose(put.astype(F32)) > 0.5)
            part = dot(pick, stiff[s]).astype(BF16)
            face_part[:, (2 * s + side) * STEP : (2 * s + side + 1) * STEP, :] = part.reshape(
                GROUP, STEP, 1024
            )

    partner = {"sub": sub, "crow": crow + 1 - 2 * core, "ccol": ccol}
    for half in range(2):
        theirs = face_part.at[pl.ds(4 * half + 2 * (1 - core), 2)]
        copy(theirs, face_pair.at[pl.ds(2 * half, 2)], *sems("pair", 0), partner)
    for s in range(2):
        local[s] = dot(linv[s], loads[s])
        wb[0, s, mine] = local[s].astype(BF16)
    to_group(lambda t: wb.at[0, :, mine], wb.at[0, :, mine], "w", 0)
    out_row, out_of = iota((128, OWN), 0), iota((128, OWN), 1)
    part_of, within = out_row // STEP, lax.rem(out_row, STEP)
    part_core = lax.rem(part_of // 2, 2)
    part_chip = (part_of // 4) * 2 + lax.rem(part_of, 2)
    wide = (out_of == part_chip * CAP + part_core * STEP + within) & (within < STEP - 8 * part_core)
    cinv_wide[...] = dot(mask(wide), cinv[...]).astype(BF16)


    def settle_faces():
        face_own[...] = face_got[0] + face_got[1] + face_got[2] + face_got[3]

    def pass_faces():
        arrived("pair", 0)
        for half in range(2):
            ours = pl.ds(4 * half + 2 * core, 2)
            face_part[ours] = face_part[ours] + face_pair[2 * half : 2 * half + 2]
        face_got[chip] = face_part[g]

        def step(k):
            other = lax.rem(chip + k, 4)
            row, column = (other // 2) * 2 + core, lax.rem(other, 2)
            device = {"sub": sub, "crow": row, "ccol": column}
            copy(face_part.at[row * 2 + column], face_got.at[chip], *sems("faces", 0), device)

        repeat(1, 4, step)

    pass_faces()
    arrived("basis", 0)
    for s in range(2):
        restricted[s * MODES : (s + 1) * MODES] = dot(
            basis_t[s * MODES : (s + 1) * MODES, :], loads[s]
        ).astype(BF16)
    rows = dot(select_own[:, 0:OWN], restricted[...]).astype(BF16)

    def spread(p, rows):
        head[(p, *spot(0))] = rows[0:HEAD]
        tail[(p, *spot(1))] = rows[HEAD:CAP]
        pipe_start(PIPES[1 + p], [head.at[p], tail.at[p]])

    spread(0, rows)
    pipe_forward("place", [place_buf])
    pipe_forward("b0", [head.at[0], tail.at[0]])

    pipe_wait("place", [place_buf])
    tall = iota((BLOCK, 128), 0).astype(F32) + 1.0
    for c in range(8):
        where = jnp.sum(place_buf[c, :, 0, 0:128], axis=0, keepdims=True)
        perm_head[:, c * 128 : (c + 1) * 128] = dot(cinv_wide[...], mask(tall == where)).astype(BF16)
    for c in range(4):
        where = jnp.sum(
            place_buf[:, 2 * c, 0, 128:256] + place_buf[:, 2 * c + 1, 0, 128:256], axis=0, keepdims=True
        )
        perm_tail[:, c * 128 : (c + 1) * 128] = dot(cinv_wide[...], mask(tall == where)).astype(BF16)
    for s in range(2):
        for j in range(8):
            shift = mask(iota((MODES, 128), 1) == iota((MODES, 128), 0) + MODES * s)
            turned = dot_tn(basis_t[s * MODES : (s + 1) * MODES, j * 128 : (j + 1) * 128], shift)
            basis_full[s, j * 128 : (j + 1) * 128, :] = turned.astype(BF16)
    select = mask(
        jnp.broadcast_to(code_lane[0:1], (GROUP * CAP, 128)) == iota((GROUP * CAP, 128), 0).astype(F32)
    )
    for s in range(2):
        keep = (iota((OWN, 128), 0) >= s * MODES) & (iota((OWN, 128), 0) < (s + 1) * MODES)
        part = jnp.where(keep, basis_own.astype(F32), 0.0).astype(BF16)
        bp[s] = dot(select[:, 0:OWN], part).astype(BF16)

    def index_of(other):
        y, z = other // SIDE, lax.rem(other, SIDE)
        a = z * (1 - core) + y * core
        b = y * (1 - core) + z * core
        return place_buf[b, a, :, 256:384]

    after_index = index_of(lax.rem(sub + 1, PLANE))
    before_index = index_of(lax.rem(sub + PLANE - 1, PLANE))
    index_near = jnp.where(lane[0:1] < MODES, after_index, before_index)
    index_near = jnp.transpose(jnp.broadcast_to(index_near, (128, 128)))
    for j in range(8):
        column = lane_i + 128 * j
        within = lax.rem(column, STEP)
        row_of = (column // STEP) * OWN + chip * CAP + core * STEP + within
        row_of = jnp.where(within < STEP - 8 * core, row_of, -5)
        for k, index in enumerate((index_down, index_near)):
            chosen = mask(index == row_of.astype(F32))[0:OWN]
            pick_coarse[k * OWN : (k + 1) * OWN, j * 128 : (j + 1) * 128] = chosen

    def coarse_start(p):
        pipe_wait(PIPES[1 + p], [head.at[p], tail.at[p]])
        part = dot(perm_head[...], head[p].reshape(PLANE * HEAD, 128))
        part += dot(perm_tail[...], tail[p].reshape(PLANE * TAIL, 128))
        sc[p] = part.reshape(GROUP, STEP, 128)
        rc[p, g] = sc[p, g]
        to_group(lambda t: sc.at[p, t], rc.at[p, g], "c", p)
        if p == 0:
            arrived("faces", 0)
            settle_faces()
            arrived("w", 0)
            faces_start(0)
        arrived("c", p)
        total = rc[p, 0]
        for t in range(1, GROUP):
            total += rc[p, t]
        gd[p, sub] = total.astype(BF16)
        s, r = sems("d", p)
        for kind, size in enumerate((16, 8)):
            @pl.when(core == kind)
            def _():
                block = gd.at[p, sub, pl.ds(0, size)]
                repeat(0, PLANE - 1, lambda k: copy(block, block, s, r, plane_peer(k)))

    def each_plane(p, which):
        for kind, size in enumerate((16, 8)):
            @pl.when(core == kind)
            def _():
                wait(gd.at[p, pl.ds(0, PLANE - 1), pl.ds(0, size)], sems("d", p)[which])

    def coarse_pick(p):
        each_plane(p, 1)
        found = dot(pick_coarse[...], gd[p].reshape(PLANE * STEP, 128))
        re[p, g] = found.astype(BF16)
        to_group(lambda t: re.at[p, g], re.at[p, g], "e", p)
    def coarse_end(p):
        arrived("e", p)
        picked = re[p, 0].astype(F32)
        for t in range(1, GROUP):
            picked += re[p, t].astype(F32)
        pk[p, 0, 0:OWN] = picked[0:OWN].astype(BF16)
        pk[p, 1, 0:OWN] = picked[OWN : 2 * OWN].astype(BF16)


    def faces_start(p):
        for kind in range(2 * p, 2 + p):
            source = basis_full if kind == 1 else wb.at[p]
            faces = [
                dot(face_own[2 * STEP * s : 2 * STEP * (s + 1)], source[s]).astype(BF16) for s in range(2)
            ]
            nb[kind, 0, g] = faces[1][0:STEP]
            nb[kind, 1, g] = faces[0][STEP : 2 * STEP]
            fs[kind, 0] = faces[0][0:STEP]
            fs[kind, 1] = faces[1][STEP : 2 * STEP]
        s_before, r_before = sems("before", p)
        s_after, r_after = sems("after", p)

        def outward(k):
            t = lax.rem(g + k, GROUP)
            place = {"crow": t // 2, "ccol": lax.rem(t, 2)}
            up = {"sub": lax.rem(sub + 1, PLANE), **place}
            low = {"sub": lax.rem(sub + PLANE - 1, PLANE), **place}
            copy(fs.at[kinds(p), 1], nb.at[kinds(p), 2, g], s_before, r_before, up)
            copy(fs.at[kinds(p), 0], nb.at[kinds(p), 3, g], s_after, r_after, low)

        repeat(0, GROUP, outward)
        inner = nb.at[kinds(p), pl.ds(0, 2), g]
        to_group(lambda t: inner, inner, "inner", p)

    def faces_wait(p):
        for stage in ("inner", "before", "after"):
            arrived(stage, p)

    def face(kind, which):
        return nb[kind, which].reshape(128, 128)

    def residual_local(p):
        kind = 2 * p
        after = (face(kind, 0), face(kind, 3))
        before = (face(kind, 2), face(kind, 1))
        return [
            loads[s, mine].astype(F32)
            - (dot(stiff[s], wb[p, s]) + dot(put_face[s, 0], before[s]) + dot(put_face[s, 1], after[s]))
            for s in range(2)
        ]

    def residual_of(p, early):
        return [early[s] - (dot(ab[s, 0], pk[p, 0]) + dot(ab[s, 1], pk[p, 1])) for s in range(2)]

    coarse_start(0)
    faces_wait(0)
    for s in range(2):
        image = dot(stiff[s], basis_full[s])
        if s == 0:
            ab[s, 0] = (image + dot(put_face[0, 1], face(1, 0))).astype(BF16)
            ab[s, 1] = dot(put_face[0, 0], face(1, 2)).astype(BF16)
        else:
            ab[s, 0] = (image + dot(put_face[1, 0], face(1, 1))).astype(BF16)
            ab[s, 1] = dot(put_face[1, 1], face(1, 3)).astype(BF16)
    early = residual_local(0)
    for s in range(2):
        kept[s] = early[s]
    pieces = [[early[s].astype(BF16) for s in range(2)]] + [[ab[s, k] for s in range(2)] for k in range(2)]
    for k, piece in enumerate(pieces):
        part = dot(bp[0], piece[0]) + dot(bp[1], piece[1])
        sa[:, k] = part.reshape(GROUP, CAP, 128)
    ra[g] = sa[g]
    to_group(lambda t: sa.at[t], ra.at[g], "a", 0)
    coarse_pick(0)
    arrived("a", 0)
    total = ra[0]
    for t in range(1, GROUP):
        total += ra[t]
    coarse_end(0)
    rows = total[0] - dot(total[1].astype(BF16), pk[0, 0]) - dot(total[2].astype(BF16), pk[0, 1])
    spread(1, rows.astype(BF16))
    residual = residual_of(0, [kept[s] for s in range(2)])
    for s in range(2):
        rf[s, mine] = residual[s].astype(BF16)
    to_group(lambda t: rf.at[:, mine], rf.at[:, mine], "r", 0)
    for s in range(2):
        first[s] = local[s] + dot(basis_full[s, mine], pk[0, 0])
    pipe_forward("b1", [head.at[1], tail.at[1]])
    arrived("r", 0)
    for s in range(2):
        first[s] = first[s] + dot(linv[s], rf[s])
        wb[1, s, mine] = first[s].astype(BF16)
    coarse_start(1)
    to_group(lambda t: wb.at[1, :, mine], wb.at[1, :, mine], "w", 1)
    coarse_pick(1)
    arrived("w", 1)
    faces_start(1)
    faces_wait(1)
    early = residual_local(1)
    coarse_end(1)
    for s in range(2):
        out[s] = first[s] + dot(basis_full[s, mine], pk[1, 0])
    final = residual_of(1, early)
    for s in range(2):
        out[2 + s] = final[s]

    for stage in ("basis", "pair", "faces", "a", "r"):
        wait(arrivals[stage](0), sems(stage, 0)[0])
    pipe_settle("place", [place_buf])
    for p in range(2):
        for stage in ("c", "e", "w", "inner", "before", "after"):
            wait(arrivals[stage](p), sems(stage, p)[0])
        each_plane(p, 0)
        pipe_settle(PIPES[1 + p], [head.at[p], tail.at[p]])


def body(loads, stiffness, local_inverse, coarse_basis, coarse_inverse, coarse_index, left, right):
    vmem = pl.BlockSpec(memory_space=pltpu.VMEM)
    away = pl.BlockSpec(memory_space=pl.ANY)
    out = jax.ShapeDtypeStruct((2, 128, 128), F32)
    count = 2 * len(STAGES)
    dma = pltpu.SemaphoreType.DMA
    both = pl.pallas_call(
        kernel,
        out_shape=jax.ShapeDtypeStruct((4, 128, 128), F32),
        in_specs=[away] * 8,
        out_specs=vmem,
        scratch_shapes=[
            pltpu.VMEM((2, 1024, 128), BF16),
            pltpu.VMEM((2, 128, 1024), BF16),
            pltpu.VMEM((2, 128, 1024), BF16),
            pltpu.VMEM((OWN, BLOCK), BF16),
            pltpu.VMEM((2, MODES), I32),
            pltpu.VMEM((2, MODES, 128), BF16),
            pltpu.VMEM((2, 128), I32),
            pltpu.VMEM((2, 128), I32),
            pltpu.VMEM((SIDE, SIDE, 1, 384), F32),
            pltpu.VMEM((128, BLOCK), BF16),
            pltpu.VMEM((128, PLANE * HEAD), BF16),
            pltpu.VMEM((128, PLANE * TAIL), BF16),
            pltpu.VMEM((2, GROUP * CAP, 128), BF16),
            pltpu.VMEM((OWN, 1024), BF16),
            pltpu.VMEM((2, 1024, 128), BF16),
            pltpu.VMEM((2, 2, 128, 128), BF16),
            pltpu.VMEM((2 * OWN, PLANE * STEP), BF16),
            pltpu.VMEM((GROUP, 4 * STEP, 1024), BF16),
            pltpu.VMEM((4, 4 * STEP, 1024), BF16),
            pltpu.VMEM((4, 4 * STEP, 1024), BF16),
            pltpu.VMEM((4 * STEP, 1024), BF16),
            pltpu.VMEM((GROUP, 3, CAP, 128), F32),
            pltpu.VMEM((GROUP, 3, CAP, 128), F32),
            pltpu.VMEM((2, SIDE, SIDE, HEAD, 128), BF16),
            pltpu.VMEM((2, SIDE, SIDE, TAIL, 128), BF16),
            pltpu.VMEM((2, GROUP, STEP, 128), F32),
            pltpu.VMEM((2, GROUP, STEP, 128), F32),
            pltpu.VMEM((2, PLANE, STEP, 128), BF16),
            pltpu.VMEM((2, GROUP, 2 * OWN, 128), BF16),
            pltpu.VMEM((2, 2, 128, 128), BF16),
            pltpu.VMEM((2, 2, 1024, 128), BF16),
            pltpu.VMEM((2, 2, 128, 128), BF16),
            pltpu.VMEM((3, 2, STEP, 128), BF16),
            pltpu.VMEM((3, 4, GROUP, STEP, 128), BF16),
            pltpu.VMEM((2, 1024, 128), BF16),
            pltpu.VMEM((2, 128, 128), F32),
            pltpu.VMEM((2, 128, 128), F32),
            pltpu.VMEM((2, 128, 128), F32),
            pltpu.VMEM((OWN, 128), BF16),
            dma((count,)),
            dma((count,)),
            dma((len(PIPES), 2, SIDE)),
            dma((len(PIPES), 2)),
            dma((len(PIPES), 2)),
            dma((len(PIPES), 2)),
            dma((8,)),
        ],
        compiler_params=pltpu.CompilerParams(collective_id=0, has_side_effects=True),
        name="schwarz",
    )(
        loads, stiffness, local_inverse, jnp.swapaxes(coarse_basis, 1, 2), coarse_inverse, coarse_index, left, right
    )
    return both[0:2], both[2:4]


def solution(mesh):
    group = ("crow", "ccol")
    return jax.shard_map(
        body,
        mesh=mesh,
        in_specs=(
            P("sub", None, None),
            P("sub", group, None),
            P("sub", group, None),
            P("sub", group, None),
            P("sub", group),
            P("sub", None),
            P("sub", None),
            P("sub", None),
        ),
        out_specs=(P("sub", group, None), P("sub", group, None)),
        check_vma=False,
    )
```
